32 devices in a mesh: groups: 2 (over y), ctx: 4 (over z), chan: 4 (over x, core).
Axes of the slice: x: 2, y: 2, z: 4, core: 2. Of those that a mesh axis runs over, the one named last changes fastest.
Arguments:
- q_feat: bfloat16 [4096, 8192], P(('groups', 'ctx'), 'chan'), parts along dimension 0, may hold values from -6 to 6
- k_feat: bfloat16 [4096, 8192], P(('groups', 'ctx'), 'chan'), parts along dimension 0, may hold values from -6 to 6
- v_feat: bfloat16 [4096, 8192], P(('groups', 'ctx'), 'chan'), parts along dimension 0, may hold values from -6 to 6
- pole_rate: float32 [16, 8192], P(None, 'chan'), may hold values from 4.8828126e-05 to 0.03
- residue: float32 [16, 8192], P(None, 'chan'), may hold values from -1.5 to 1.5
- skip_gain: float32 [8192], P('chan'), may hold values from 0.5 to 1.5
- lengths: int32 [8], P('groups'), parts along dimension 0, may hold values from 1 to 1024, 2048 in all
- owners: int32 [8], P('groups'), parts along dimension 0, may hold values from 0 to 3, as said below
Outputs:
- mixed_out: bfloat16 [4096, 8192], P(('groups', 'ctx'), 'chan'), parts along dimension 0
- decode_state: float32 [8, 16, 8192], P(('groups', 'ctx'), None, 'chan'), parts along dimension 0
The draws below stay inside these ranges and needn't reach their ends.
There are 2 independent parts, one for each index of `groups`. The reference program is written for one: setup_inputs(seed, part) draws one part's arguments, and reference() takes and returns one part's arrays. A program takes and returns all parts, laid end to end along the dimension named above; an argument that names none is the same for every part. Nothing has to cross between parts.
Inputs may be any that keep to these rules, and one draw needn't show every extreme that they name: The 4 lengths sum to 2048; the longest is exactly 1024. The 4 owners are distinct.
All inputs are finite; a program needn't handle non-finite values.
Results may differ from the reference program's by a relative error of at most 0.001.
Values sent between devices are 32-bit elements; how exact they have to be, the bound alone decides.
A program may use at most 128 MiB of HBM per device.

```python
import math
import jax
import jax.numpy as jnp
import numpy as np
from jax import lax

D = 8192
POLES = 16
REQS = 4
TOKENS = 2048
OWNER_SLOTS = 4
N_CTX = 4


def draw_owners(key, part):
    middle = 1 + jax.random.permutation(jax.random.fold_in(key, 17), N_CTX - 2)[:REQS - 2]
    values = jnp.concatenate([jnp.array([N_CTX - 1, 0], jnp.int32), middle.astype(jnp.int32)])
    order = jax.random.permutation(jax.random.fold_in(key, 23), REQS)
    return values[order].astype(jnp.int32)


def block_levels(rng, dims, shards, smallest, top_value):
    factor_of, own = 1.0, jax.random.fold_in(rng, 6)
    for dim, parts in shards:
        draws = jnp.exp(jax.random.uniform(jax.random.fold_in(own, dim), (parts,), jnp.float32, smallest / len(shards), top_value / len(shards)))
        factor_of = factor_of * jnp.repeat(draws, dims[dim] // parts).reshape([-1 if axis == dim else 1 for axis in range(len(dims))])
    return factor_of


def length_profile(amount, total, most, slope):
    loads = [(1 << 20) // math.isqrt(standing ** slope) + 1 for standing in range(2, amount + 1)]
    spare, holding = total - most - (amount - 1), [1] * (amount - 1)
    while spare > 0:
        free = [i for i in range(amount - 1) if holding[i] < most]
        whole, remaining = sum([loads[i] for i in free]), spare
        for i in free:
            more = min(most - holding[i], max(1, remaining * loads[i] // whole), spare)
            holding[i] = holding[i] + more
            spare = spare - more
    return np.array([most] + holding)


def ragged_sizes(stream_key, number_of, total, most, lean):
    if number_of == 2:
        one = jax.random.randint(stream_key, (), max(1, total - most), min(most, total - 1) + 1)
        return jnp.stack([one, total - one])
    sizes = jnp.asarray(length_profile(number_of, total, most, lean), jnp.int32)
    twos = (number_of - 1) // 2
    giver, receiver = sizes[1:1 + 2 * twos:2], sizes[2:2 + 2 * twos:2]
    margin = jnp.minimum(giver - 1, most - receiver)
    moved = jax.random.randint(jax.random.fold_in(stream_key, 1), (twos,), 0, 1 << 20) % (margin + 1)
    sizes = sizes.at[1:1 + 2 * twos:2].set(giver - moved).at[2:2 + 2 * twos:2].set(receiver + moved)
    return sizes[jax.random.permutation(jax.random.fold_in(stream_key, 2), number_of)]


def centred(rng, extent, width, most, pieces=(), held_as=jnp.bfloat16):
    values = width * jax.random.normal(rng, extent, jnp.float32)
    if pieces:
        values = values * block_levels(rng, extent, pieces, -0.22, 0.18)
    return jnp.clip(values, -most, most).astype(held_as)


def setup_inputs(seed: int = 0, part: int = 0) -> dict:
    splits = jax.random.split(jax.random.key(seed), 9)
    part_splits = jax.random.split(jax.random.fold_in(splits[8], part), 9)
    q_feat = centred(part_splits[0], (TOKENS, D), 1.0, 6.0, ((0, 4), (1, 4)))
    k_feat = centred(part_splits[1], (TOKENS, D), 1.0, 6.0, ((0, 4), (1, 4)))
    v_feat = centred(part_splits[2], (TOKENS, D), 1.0, 6.0, ((0, 4), (1, 4)))
    pole_rate = jnp.clip(jnp.exp(math.log(0.03) - 6.420646 * jax.random.uniform(splits[3], (POLES, D), jnp.float32) ** block_levels(splits[3], (POLES, D), ((1, 4),), -0.2, 0.2)), 4.882812572759576e-05, 0.03)
    residue = centred(splits[4], (POLES, D), 0.25, 1.5, ((1, 4),), jnp.float32)
    skip_gain = jnp.clip(0.5 + 1.0 * jax.random.uniform(splits[5], (D,), jnp.float32) ** block_levels(splits[5], (D,), ((0, 4),), -0.2, 0.2), 0.5, 1.5)
    lengths = ragged_sizes(part_splits[6], REQS, TOKENS, TOKENS // 2, 2).astype(jnp.int32)
    owners = draw_owners(jax.random.fold_in(jax.random.fold_in(splits[8], part), 71), part)
    return dict(q_feat=q_feat, k_feat=k_feat, v_feat=v_feat, pole_rate=pole_rate, residue=residue, skip_gain=skip_gain, lengths=lengths, owners=owners)


def reference(q_feat, k_feat, v_feat, pole_rate, residue, skip_gain, lengths, owners):
    mixed_in = k_feat.astype(jnp.float32) * v_feat.astype(jnp.float32)
    offsets = (jnp.cumsum(lengths) - lengths).astype(jnp.int32)
    positions = jnp.arange(TOKENS, dtype=jnp.int32)
    segment = (lax.optimization_barrier(jnp.sum((positions[:, None] >= offsets[None, :]).astype(jnp.int32), axis=1)) - 1).astype(jnp.int32)
    is_start = positions == offsets[segment]
    pole_decay = jnp.exp(-pole_rate)
    scaled_res = residue * jnp.sqrt(1.0 - jnp.exp(-2.0 * pole_rate))

    def advance(loop_carry, inputs_now):
        mode_state, store = loop_carry
        row_in, seg_now, start_now = inputs_now
        mode_state = jnp.where(start_now, jnp.zeros_like(mode_state), pole_decay * mode_state) + row_in[None, :]
        store = store.at[seg_now].set(mode_state)
        return ((mode_state, store), lax.optimization_barrier(jnp.sum(scaled_res * mode_state, axis=0)))
    init_state = jnp.zeros((POLES, D), jnp.float32)
    init_store = jnp.zeros((REQS, POLES, D), jnp.float32)
    (last_state, store), conv = lax.scan(advance, (init_state, init_store), (mixed_in, segment, is_start))
    mixed_out = (q_feat.astype(jnp.float32) * (conv + skip_gain[None, :] * mixed_in)).astype(jnp.bfloat16)
    decode_state = jnp.zeros((OWNER_SLOTS, POLES, D), jnp.float32).at[owners.astype(jnp.int32)].set(store)
    return (mixed_out, decode_state)
```

```python
import functools

import jax
import jax.numpy as jnp
from jax import lax
from jax.experimental import pallas as pl
from jax.experimental.pallas import tpu as pltpu
from jax.sharding import PartitionSpec as P

F32 = jnp.float32
LANES = 128
ROWS = 8
UNROLL = 8


def spans(lens_ref, count, tok):
    first = lax.axis_index("ctx") * tok
    offset = jnp.int32(0)
    found = []
    for r in range(count):
        size = lens_ref[r]
        end = offset + size
        lo = jnp.clip(offset - first, 0, tok)
        hi = jnp.clip(end - first, 0, tok)
        found.append((lo, hi, offset < first, end > first, end <= first + tok, end - first))
        offset = end
    return found


def spread(value, dst_ref, sub, base=0):
    for i in range(value.shape[0] // ROWS):
        for j in range(sub):
            dst_ref[pl.ds(base + i * ROWS * sub + j, ROWS, stride=sub), :] = value[
                i * ROWS : (i + 1) * ROWS, j * LANES : (j + 1) * LANES
            ]


def unspread(src_ref, dst_ref, count, sub):
    for i in range(count // ROWS):
        for j in range(sub):
            dst_ref[i * ROWS : (i + 1) * ROWS, j * LANES : (j + 1) * LANES] = src_ref[
                pl.ds(i * ROWS * sub + j, ROWS, stride=sub), :
            ]


def walk(lo, hi, step, state):
    groups = (hi - lo) // UNROLL

    def many(i, state):
        start = lo + i * UNROLL
        for k in range(UNROLL):
            state = step(start + k, state)
        return state

    state = lax.fori_loop(0, groups, many, state)
    return lax.fori_loop(lo + groups * UNROLL, hi, step, state)


def ends_kernel(
    lens_ref, own_ref, k_ref, v_ref, rate_ref, u_ref, end_ref, span_ref, base_ref, coef_ref,
    decay_sc, state_sc, *, tok, sub, poles, count, chunk,
):
    rate = rate_ref[...]
    spread(jnp.exp(-rate), decay_sc, sub)

    def mix(i, _):
        start = pl.multiple_of(i * chunk, chunk)
        u = k_ref[pl.ds(start, chunk), :].astype(F32) * v_ref[pl.ds(start, chunk), :].astype(F32)
        spread(u, u_ref, sub, start * sub)
        return 0

    lax.fori_loop(0, tok // chunk, mix, 0)
    decay = [decay_sc[p * sub : (p + 1) * sub, :] for p in range(poles)]

    def step(t, state):
        u = u_ref[pl.ds(pl.multiple_of(t * sub, sub), sub), :]
        return tuple(d * s + u for d, s in zip(decay, state))

    base_ref[...] = jnp.zeros_like(base_ref)
    coef_ref[...] = jnp.zeros_like(coef_ref)
    span_ref[...] = jnp.zeros_like(span_ref)
    zero = tuple(jnp.zeros((sub, LANES), F32) for _ in range(poles))
    for r, (lo, hi, before, reaches, ends, steps) in enumerate(spans(lens_ref, count, tok)):

        @pl.when(hi > lo)
        def _():
            state = walk(lo, hi, step, zero)
            for p in range(poles):
                state_sc[p * sub : (p + 1) * sub, :] = state[p]

            @pl.when(hi == tok)
            def _():
                unspread(state_sc, end_ref, poles, sub)

            @pl.when(ends)
            def _():
                unspread(state_sc, base_ref.at[own_ref[r]], poles, sub)

            @pl.when(before & ends)
            def _():
                coef_ref[own_ref[r]] = jnp.exp(rate * -steps.astype(F32))

            @pl.when(before & (hi == tok))
            def _():
                span_ref[...] = jnp.exp(rate * -float(tok))


def conv_kernel(
    lens_ref, u_ref, q_ref, rate_ref, res_ref, gain_ref, in_ref, out_ref,
    decay_sc, res_sc, state_sc, gain_sc, conv_sc, *, tok, sub, poles, count, chunk,
):
    rate = rate_ref[...]
    spread(jnp.exp(-rate), decay_sc, sub)
    spread(res_ref[...] * jnp.sqrt(1.0 - jnp.exp(-2.0 * rate)), res_sc, sub)
    for j in range(sub):
        gain_sc[j : j + 1, :] = gain_ref[0:1, j * LANES : (j + 1) * LANES]
    decay = [decay_sc[p * sub : (p + 1) * sub, :] for p in range(poles)]
    scale = [res_sc[p * sub : (p + 1) * sub, :] for p in range(poles)]
    gain = gain_sc[...]

    def step(t, state):
        rows = pl.ds(pl.multiple_of(t * sub, sub), sub)
        u = u_ref[rows, :]
        state = tuple(d * s + u for d, s in zip(decay, state))
        terms = [gain * u] + [c * s for c, s in zip(scale, state)]
        while len(terms) > 1:
            terms = [a + b for a, b in zip(terms[::2], terms[1::2])] + (
                [terms[-1]] if len(terms) % 2 else []
            )
        conv_sc[rows, :] = terms[0]
        return state

    for lo, hi, before, reaches, ends, steps in spans(lens_ref, count, tok):

        @pl.when(hi > lo)
        def _():
            @pl.when(before)
            def _():
                spread(in_ref[...], state_sc, sub)

            @pl.when(jnp.logical_not(before))
            def _():
                state_sc[...] = jnp.zeros_like(state_sc)

            state = tuple(state_sc[p * sub : (p + 1) * sub, :] for p in range(poles))
            walk(lo, hi, step, state)

    def gate(i, _):
        start = pl.multiple_of(i * chunk, chunk)
        rows = pl.ds(start, chunk)
        for j in range(sub):
            lanes = slice(j * LANES, (j + 1) * LANES)
            conv = conv_sc[pl.ds(start * sub + j, chunk, stride=sub), :]
            out_ref[rows, lanes] = (q_ref[rows, lanes].astype(F32) * conv).astype(out_ref.dtype)
        return 0

    lax.fori_loop(0, tok // chunk, gate, 0)


def shards(q_feat, k_feat, v_feat, pole_rate, residue, skip_gain, lengths, owners):
    tok, channels = q_feat.shape
    poles, count = pole_rate.shape[0], lengths.shape[0]
    slots = lax.axis_size("ctx")
    sub = min(ROWS, channels // LANES)
    width = sub * LANES
    tiles = channels // width
    sizes = dict(tok=tok, sub=sub, poles=poles, count=count, chunk=16)
    feat = pl.BlockSpec((tok, width), lambda i, *_: (0, i))
    pole = pl.BlockSpec((poles, width), lambda i, *_: (0, i))
    slot = pl.BlockSpec((slots, poles, width), lambda i, *_: (0, 0, i))
    flat = pl.BlockSpec((tok * sub, LANES), lambda i, *_: (i, 0))
    small = pltpu.VMEM((poles * sub, LANES), F32)
    elems = tok * channels
    mixed, end, span, base, coef = pl.pallas_call(
        functools.partial(ends_kernel, **sizes),
        grid_spec=pltpu.PrefetchScalarGridSpec(
            num_scalar_prefetch=2,
            grid=(tiles,),
            in_specs=[feat, feat, pole],
            out_specs=[flat, pole, pole, slot, slot],
            scratch_shapes=[small, small],
        ),
        out_shape=[
            jax.ShapeDtypeStruct((tiles * tok * sub, LANES), F32),
            jax.ShapeDtypeStruct((poles, channels), F32),
            jax.ShapeDtypeStruct((poles, channels), F32),
            jax.ShapeDtypeStruct((slots, poles, channels), F32),
            jax.ShapeDtypeStruct((slots, poles, channels), F32),
        ],
        cost_estimate=pl.CostEstimate(
            flops=2 * poles * elems, bytes_accessed=8 * elems, transcendentals=0
        ),
        name="ends",
    )(lengths, owners, k_feat, v_feat, pole_rate)

    longest = tok * slots // 2
    hops = min((longest - 2) // tok + 1, slots - 1)
    route = [(i, i + 1) for i in range(slots - 1)]
    incoming = lax.ppermute(end, "ctx", route)
    for _ in range(hops - 1):
        incoming = lax.ppermute(span * incoming + end, "ctx", route)
    slotted = base + coef * incoming[None]
    received = lax.all_to_all(
        slotted.reshape(slots, 1, poles, channels), "ctx", split_axis=0, concat_axis=0, tiled=True
    )
    decode_state = jnp.sum(received, axis=0)

    mixed_out = pl.pallas_call(
        functools.partial(conv_kernel, **sizes),
        grid_spec=pltpu.PrefetchScalarGridSpec(
            num_scalar_prefetch=1,
            grid=(tiles,),
            in_specs=[
                flat, feat, pole, pole, pl.BlockSpec((1, width), lambda i, *_: (0, i)), pole
            ],
            out_specs=feat,
            scratch_shapes=[
                small, small, small, pltpu.VMEM((sub, LANES), F32),
                pltpu.VMEM((tok * sub, LANES), F32),
            ],
        ),
        out_shape=jax.ShapeDtypeStruct((tok, channels), q_feat.dtype),
        cost_estimate=pl.CostEstimate(
            flops=8 * poles * elems, bytes_accessed=8 * elems, transcendentals=0
        ),
        name="conv",
    )(lengths, mixed, q_feat, pole_rate, residue, skip_gain[None, :], incoming)
    return mixed_out, decode_state


def solution(mesh):
    tokens = P(("groups", "ctx"), "chan")
    return jax.shard_map(
        shards,
        mesh=mesh,
        in_specs=(
            tokens, tokens, tokens, P(None, "chan"), P(None, "chan"), P("chan"),
            P("groups"), P("groups"),
        ),
        out_specs=(tokens, P(("groups", "ctx"), None, "chan")),
        check_vma=False,
    )
```

```python
import functools

import jax
import jax.numpy as jnp
from jax import lax
from jax.experimental import pallas as pl
from jax.experimental.pallas import tpu as pltpu
from jax.sharding import PartitionSpec as P

F32 = jnp.float32
LANES = 128
ROWS = 8
UNROLL = 8


def spans(lens_ref, count, tok):
    first = lax.axis_index("ctx") * tok
    offset = jnp.int32(0)
    found = []
    for r in range(count):
        size = lens_ref[r]
        end = offset + size
        lo = jnp.clip(offset - first, 0, tok)
        hi = jnp.clip(end - first, 0, tok)
        found.append((lo, hi, offset < first, end > first, end <= first + tok, end - first))
        offset = end
    return found


def spread(value, dst_ref, sub, base=0):
    for i in range(value.shape[0] // ROWS):
        for j in range(sub):
            dst_ref[pl.ds(base + i * ROWS * sub + j, ROWS, stride=sub), :] = value[
                i * ROWS : (i + 1) * ROWS, j * LANES : (j + 1) * LANES
            ]


def unspread(src_ref, dst_ref, count, sub):
    for i in range(count // ROWS):
        for j in range(sub):
            dst_ref[i * ROWS : (i + 1) * ROWS, j * LANES : (j + 1) * LANES] = src_ref[
                pl.ds(i * ROWS * sub + j, ROWS, stride=sub), :
            ]


def walk(lo, hi, step, state):
    groups = (hi - lo) // UNROLL

    def many(i, state):
        start = lo + i * UNROLL
        for k in range(UNROLL):
            state = step(start + k, state)
        return state

    state = lax.fori_loop(0, groups, many, state)
    return lax.fori_loop(lo + groups * UNROLL, hi, step, state)


def ends_kernel(
    lens_ref, own_ref, k_ref, v_ref, rate_ref, u_ref, end_ref, span_ref, base_ref, coef_ref,
    decay_sc, state_sc, *, tok, sub, poles, count, chunk,
):
    rate = rate_ref[...]
    spread(jnp.exp(-rate), decay_sc, sub)

    def mix(i, _):
        start = pl.multiple_of(i * chunk, chunk)
        u = k_ref[pl.ds(start, chunk), :].astype(F32) * v_ref[pl.ds(start, chunk), :].astype(F32)
        spread(u, u_ref, sub, start * sub)
        return 0

    lax.fori_loop(0, tok // chunk, mix, 0)
    decay = [decay_sc[p * sub : (p + 1) * sub, :] for p in range(poles)]

    def step(t, state):
        u = u_ref[pl.ds(pl.multiple_of(t * sub, sub), sub), :]
        return tuple(d * s + u for d, s in zip(decay, state))

    base_ref[...] = jnp.zeros_like(base_ref)
    coef_ref[...] = jnp.zeros_like(coef_ref)
    span_ref[...] = jnp.zeros_like(span_ref)
    zero = tuple(jnp.zeros((sub, LANES), F32) for _ in range(poles))
    for r, (lo, hi, before, reaches, ends, steps) in enumerate(spans(lens_ref, count, tok)):

        @pl.when(hi > lo)
        def _():
            state = walk(lo, hi, step, zero)
            for p in range(poles):
                state_sc[p * sub : (p + 1) * sub, :] = state[p]

            @pl.when(hi == tok)
            def _():
                unspread(state_sc, end_ref, poles, sub)

            @pl.when(ends)
            def _():
                unspread(state_sc, base_ref.at[own_ref[r]], poles, sub)

            @pl.when(before & ends)
            def _():
                coef_ref[own_ref[r]] = jnp.exp(rate * -steps.astype(F32))

            @pl.when(before & (hi == tok))
            def _():
                span_ref[...] = jnp.exp(rate * -float(tok))


def relay_kernel(
    end_ref, span_ref, base_ref, coef_ref, in_ref, got_ref,
    arrived, passed, slotted, landed, sent_sem, come_sem, give_sem, take_sem,
    *, hops, parts,
):
    slots, _, channels = base_ref.shape
    width = channels // parts
    me = lax.axis_index("ctx")
    barrier = pltpu.get_barrier_semaphore()
    peers = [lax.rem(me + j, slots) for j in range(1, slots)]
    for peer in peers:
        pl.semaphore_signal(
            barrier, inc=1, device_id={"ctx": peer}, device_id_type=pl.DeviceIdType.MESH
        )
    pl.semaphore_wait(barrier, slots - 1)

    def lanes(part):
        return pl.ds(part * width, width)

    def pass_on(hop, part):
        source = end_ref if hop == 0 else passed.at[hop - 1]
        return pltpu.make_async_remote_copy(
            src_ref=source.at[:, lanes(part)],
            dst_ref=arrived.at[hop, :, lanes(part)],
            send_sem=sent_sem.at[hop, part],
            recv_sem=come_sem.at[hop, part],
            device_id={"ctx": lax.rem(me + 1, slots)},
            device_id_type=pl.DeviceIdType.MESH,
        )

    def give(j, part):
        return pltpu.make_async_remote_copy(
            src_ref=slotted.at[j - 1, :, lanes(part)],
            dst_ref=landed.at[j - 1, :, lanes(part)],
            send_sem=give_sem.at[j - 1, part],
            recv_sem=take_sem.at[j - 1, part],
            device_id={"ctx": peers[j - 1]},
            device_id_type=pl.DeviceIdType.MESH,
        )

    @pl.when(me == 0)
    def _():
        arrived[...] = jnp.zeros_like(arrived)

    for hop in range(hops):
        for part in range(parts):
            if hop:

                @pl.when(me > 0)
                def _():
                    pass_on(hop - 1, part).wait_recv()

                at = lanes(part)
                passed[hop - 1, :, at] = (
                    span_ref[:, at] * arrived[hop - 1, :, at] + end_ref[:, at]
                )

            @pl.when(me < slots - 1)
            def _():
                pass_on(hop, part).start()

    for part in range(parts):

        @pl.when(me > 0)
        def _():
            pass_on(hops - 1, part).wait_recv()

        at = lanes(part)
        incoming = arrived[hops - 1, :, at]
        in_ref[:, at] = incoming
        for j in range(1, slots):
            slotted[j - 1, :, at] = (
                base_ref[peers[j - 1], :, at] + coef_ref[peers[j - 1], :, at] * incoming
            )
            give(j, part).start()
        got_ref[:, at] = base_ref[me, :, at] + coef_ref[me, :, at] * incoming

    for part in range(parts):
        at = lanes(part)
        for j in range(1, slots):
            give(j, part).wait_recv()
        total = got_ref[:, at]
        for j in range(1, slots):
            total += landed[j - 1, :, at]
        got_ref[:, at] = total
    for part in range(parts):
        for j in range(1, slots):
            give(j, part).wait_send()

    @pl.when(me < slots - 1)
    def _():
        for hop in range(hops):
            for part in range(parts):
                pass_on(hop, part).wait_send()


def conv_kernel(
    lens_ref, u_ref, q_ref, rate_ref, res_ref, gain_ref, in_ref, got_ref, out_ref, kept_ref,
    decay_sc, res_sc, state_sc, gain_sc, conv_sc, *, tok, sub, poles, count, chunk,
):
    rate = rate_ref[...]
    spread(jnp.exp(-rate), decay_sc, sub)
    spread(res_ref[...] * jnp.sqrt(1.0 - jnp.exp(-2.0 * rate)), res_sc, sub)
    for j in range(sub):
        gain_sc[j : j + 1, :] = gain_ref[0:1, j * LANES : (j + 1) * LANES]
    kept_ref[0] = got_ref[...]
    decay = [decay_sc[p * sub : (p + 1) * sub, :] for p in range(poles)]
    scale = [res_sc[p * sub : (p + 1) * sub, :] for p in range(poles)]
    gain = gain_sc[...]

    def step(t, state):
        rows = pl.ds(pl.multiple_of(t * sub, sub), sub)
        u = u_ref[rows, :]
        state = tuple(d * s + u for d, s in zip(decay, state))
        terms = [gain * u] + [c * s for c, s in zip(scale, state)]
        while len(terms) > 1:
            terms = [a + b for a, b in zip(terms[::2], terms[1::2])] + (
                [terms[-1]] if len(terms) % 2 else []
            )
        conv_sc[rows, :] = terms[0]
        return state

    for lo, hi, before, reaches, ends, steps in spans(lens_ref, count, tok):

        @pl.when(hi > lo)
        def _():
            @pl.when(before)
            def _():
                spread(in_ref[...], state_sc, sub)

            @pl.when(jnp.logical_not(before))
            def _():
                state_sc[...] = jnp.zeros_like(state_sc)

            state = tuple(state_sc[p * sub : (p + 1) * sub, :] for p in range(poles))
            walk(lo, hi, step, state)

    def gate(i, _):
        start = pl.multiple_of(i * chunk, chunk)
        rows = pl.ds(start, chunk)
        for j in range(sub):
            lanes = slice(j * LANES, (j + 1) * LANES)
            conv = conv_sc[pl.ds(start * sub + j, chunk, stride=sub), :]
            out_ref[rows, lanes] = (q_ref[rows, lanes].astype(F32) * conv).astype(out_ref.dtype)
        return 0

    lax.fori_loop(0, tok // chunk, gate, 0)


def shards(q_feat, k_feat, v_feat, pole_rate, residue, skip_gain, lengths, owners):
    tok, channels = q_feat.shape
    poles, count = pole_rate.shape[0], lengths.shape[0]
    slots = lax.axis_size("ctx")
    sub = min(ROWS, channels // LANES)
    width = sub * LANES
    tiles = channels // width
    sizes = dict(tok=tok, sub=sub, poles=poles, count=count, chunk=16)
    feat = pl.BlockSpec((tok, width), lambda i, *_: (0, i))
    pole = pl.BlockSpec((poles, width), lambda i, *_: (0, i))
    slot = pl.BlockSpec((slots, poles, width), lambda i, *_: (0, 0, i))
    flat = pl.BlockSpec((tok * sub, LANES), lambda i, *_: (i, 0))
    small = pltpu.VMEM((poles * sub, LANES), F32)
    elems = tok * channels
    mixed, end, span, base, coef = pl.pallas_call(
        functools.partial(ends_kernel, **sizes),
        grid_spec=pltpu.PrefetchScalarGridSpec(
            num_scalar_prefetch=2,
            grid=(tiles,),
            in_specs=[feat, feat, pole],
            out_specs=[flat, pole, pole, slot, slot],
            scratch_shapes=[small, small],
        ),
        out_shape=[
            jax.ShapeDtypeStruct((tiles * tok * sub, LANES), F32),
            jax.ShapeDtypeStruct((poles, channels), F32),
            jax.ShapeDtypeStruct((poles, channels), F32),
            jax.ShapeDtypeStruct((slots, poles, channels), F32),
            jax.ShapeDtypeStruct((slots, poles, channels), F32),
        ],
        cost_estimate=pl.CostEstimate(
            flops=2 * poles * elems, bytes_accessed=8 * elems, transcendentals=0
        ),
        name="ends",
    )(lengths, owners, k_feat, v_feat, pole_rate)

    longest = tok * slots // 2
    hops = min((longest - 2) // tok + 1, slots - 1)
    parts = max(1, min(4, channels // LANES))
    dma = pltpu.SemaphoreType.DMA
    incoming, got = pl.pallas_call(
        functools.partial(relay_kernel, hops=hops, parts=parts),
        in_specs=[pl.BlockSpec(memory_space=pltpu.VMEM)] * 4,
        out_specs=[pl.BlockSpec(memory_space=pltpu.VMEM)] * 2,
        out_shape=[jax.ShapeDtypeStruct((poles, channels), F32)] * 2,
        scratch_shapes=[
            pltpu.VMEM((hops, poles, channels), F32),
            pltpu.VMEM((max(hops - 1, 1), poles, channels), F32),
            pltpu.VMEM((slots - 1, poles, channels), F32),
            pltpu.VMEM((slots - 1, poles, channels), F32),
            dma((hops, parts)), dma((hops, parts)),
            dma((slots - 1, parts)), dma((slots - 1, parts)),
        ],
        compiler_params=pltpu.CompilerParams(collective_id=0, has_side_effects=True),
        name="relay",
    )(end, span, base, coef)

    mixed_out, decode_state = pl.pallas_call(
        functools.partial(conv_kernel, **sizes),
        grid_spec=pltpu.PrefetchScalarGridSpec(
            num_scalar_prefetch=1,
            grid=(tiles,),
            in_specs=[
                flat, feat, pole, pole, pl.BlockSpec((1, width), lambda i, *_: (0, i)), pole,
                pole,
            ],
            out_specs=[feat, pl.BlockSpec((1, poles, width), lambda i, *_: (0, 0, i))],
            scratch_shapes=[
                small, small, small, pltpu.VMEM((sub, LANES), F32),
                pltpu.VMEM((tok * sub, LANES), F32),
            ],
        ),
        out_shape=[
            jax.ShapeDtypeStruct((tok, channels), q_feat.dtype),
            jax.ShapeDtypeStruct((1, poles, channels), F32),
        ],
        cost_estimate=pl.CostEstimate(
            flops=8 * poles * elems, bytes_accessed=8 * elems, transcendentals=0
        ),
        name="conv",
    )(lengths, mixed, q_feat, pole_rate, residue, skip_gain[None, :], incoming, got)
    return mixed_out, decode_state


def solution(mesh):
    tokens = P(("groups", "ctx"), "chan")
    return jax.shard_map(
        shards,
        mesh=mesh,
        in_specs=(
            tokens, tokens, tokens, P(None, "chan"), P(None, "chan"), P("chan"),
            P("groups"), P("groups"),
        ),
        out_specs=(tokens, P(("groups", "ctx"), None, "chan")),
        check_vma=False,
    )
```

```python
import functools

import jax
import jax.numpy as jnp
from jax import lax
from jax.experimental import pallas as pl
from jax.experimental.pallas import tpu as pltpu
from jax.sharding import PartitionSpec as P

F32 = jnp.float32
LANES = 128
ROWS = 8
UNROLL = 8


def spans(lens_ref, count, tok):
    first = lax.axis_index("ctx") * tok
    offset = jnp.int32(0)
    found = []
    for r in range(count):
        size = lens_ref[r]
        end = offset + size
        lo = jnp.clip(offset - first, 0, tok)
        hi = jnp.clip(end - first, 0, tok)
        found.append((lo, hi, offset < first, end > first, end <= first + tok, end - first))
        offset = end
    return found


def spread(value, dst_ref, sub, base=0):
    for i in range(value.shape[0] // ROWS):
        for j in range(sub):
            dst_ref[pl.ds(base + i * ROWS * sub + j, ROWS, stride=sub), :] = value[
                i * ROWS : (i + 1) * ROWS, j * LANES : (j + 1) * LANES
            ]


def unspread(src_ref, dst_ref, count, sub):
    for i in range(count // ROWS):
        for j in range(sub):
            dst_ref[i * ROWS : (i + 1) * ROWS, j * LANES : (j + 1) * LANES] = src_ref[
                pl.ds(i * ROWS * sub + j, ROWS, stride=sub), :
            ]


def walk(lo, hi, step, state):
    groups = (hi - lo) // UNROLL

    def many(i, state):
        start = lo + i * UNROLL
        for k in range(UNROLL):
            state = step(start + k, state)
        return state

    state = lax.fori_loop(0, groups, many, state)
    return lax.fori_loop(lo + groups * UNROLL, hi, step, state)


def ends_kernel(
    lens_ref, own_ref, k_ref, v_ref, rate_ref, u_ref, end_ref, span_ref, base_ref, coef_ref,
    decay_sc, state_sc, *, tok, sub, poles, count, chunk,
):
    rate = rate_ref[...]
    spread(jnp.exp(-rate), decay_sc, sub)

    def mix(i, _):
        start = pl.multiple_of(i * chunk, chunk)
        u = k_ref[pl.ds(start, chunk), :].astype(F32) * v_ref[pl.ds(start, chunk), :].astype(F32)
        spread(u, u_ref, sub, start * sub)
        return 0

    lax.fori_loop(0, tok // chunk, mix, 0)
    decay = [decay_sc[p * sub : (p + 1) * sub, :] for p in range(poles)]

    def step(t, state):
        u = u_ref[pl.ds(pl.multiple_of(t * sub, sub), sub), :]
        return tuple(d * s + u for d, s in zip(decay, state))

    base_ref[...] = jnp.zeros_like(base_ref)
    coef_ref[...] = jnp.zeros_like(coef_ref)
    span_ref[...] = jnp.zeros_like(span_ref)
    zero = tuple(jnp.zeros((sub, LANES), F32) for _ in range(poles))
    for r, (lo, hi, before, reaches, ends, steps) in enumerate(spans(lens_ref, count, tok)):

        @pl.when(hi > lo)
        def _():
            state = walk(lo, hi, step, zero)
            for p in range(poles):
                state_sc[p * sub : (p + 1) * sub, :] = state[p]

            @pl.when(hi == tok)
            def _():
                unspread(state_sc, end_ref, poles, sub)

            @pl.when(ends)
            def _():
                unspread(state_sc, base_ref.at[own_ref[r]], poles, sub)

            @pl.when(before & ends)
            def _():
                coef_ref[own_ref[r]] = jnp.exp(rate * -steps.astype(F32))

            @pl.when(before & (hi == tok))
            def _():
                span_ref[...] = jnp.exp(rate * -float(tok))


def relay_kernel(
    end_ref, span_ref, base_ref, coef_ref, in_ref, got_ref,
    arrived, passed, sent_sem, come_sem,
    *, hops, parts,
):
    slots, _, channels = base_ref.shape
    width = channels // parts
    me = lax.axis_index("ctx")
    barrier = pltpu.get_barrier_semaphore()
    for peer in (lax.rem(me + 1, slots), lax.rem(me + slots - 1, slots)):
        pl.semaphore_signal(
            barrier, inc=1, device_id={"ctx": peer}, device_id_type=pl.DeviceIdType.MESH
        )
    pl.semaphore_wait(barrier, 2)

    def lanes(part):
        return pl.ds(part * width, width)

    def pass_on(hop, part):
        source = end_ref if hop == 0 else passed.at[hop - 1]
        return pltpu.make_async_remote_copy(
            src_ref=source.at[:, lanes(part)],
            dst_ref=arrived.at[hop, :, lanes(part)],
            send_sem=sent_sem.at[hop, part],
            recv_sem=come_sem.at[hop, part],
            device_id={"ctx": lax.rem(me + 1, slots)},
            device_id_type=pl.DeviceIdType.MESH,
        )

    @pl.when(me == 0)
    def _():
        arrived[...] = jnp.zeros_like(arrived)

    for hop in range(hops):
        for part in range(parts):
            if hop:

                @pl.when(me > 0)
                def _():
                    pass_on(hop - 1, part).wait_recv()

                at = lanes(part)
                passed[hop - 1, :, at] = (
                    span_ref[:, at] * arrived[hop - 1, :, at] + end_ref[:, at]
                )

            @pl.when(me < slots - 1)
            def _():
                pass_on(hop, part).start()

    for part in range(parts):

        @pl.when(me > 0)
        def _():
            pass_on(hops - 1, part).wait_recv()

        at = lanes(part)
        incoming = arrived[hops - 1, :, at]
        in_ref[:, at] = incoming
        for q in range(slots):
            got_ref[q, :, at] = base_ref[q, :, at] + coef_ref[q, :, at] * incoming

    @pl.when(me < slots - 1)
    def _():
        for hop in range(hops):
            for part in range(parts):
                pass_on(hop, part).wait_send()


def conv_kernel(
    lens_ref, u_ref, q_ref, rate_ref, res_ref, gain_ref, in_ref, out_ref,
    decay_sc, res_sc, state_sc, gain_sc, conv_sc, *, tok, sub, poles, count, chunk,
):
    rate = rate_ref[...]
    spread(jnp.exp(-rate), decay_sc, sub)
    spread(res_ref[...] * jnp.sqrt(1.0 - jnp.exp(-2.0 * rate)), res_sc, sub)
    for j in range(sub):
        gain_sc[j : j + 1, :] = gain_ref[0:1, j * LANES : (j + 1) * LANES]
    decay = [decay_sc[p * sub : (p + 1) * sub, :] for p in range(poles)]
    scale = [res_sc[p * sub : (p + 1) * sub, :] for p in range(poles)]
    gain = gain_sc[...]

    def step(t, state):
        rows = pl.ds(pl.multiple_of(t * sub, sub), sub)
        u = u_ref[rows, :]
        state = tuple(d * s + u for d, s in zip(decay, state))
        terms = [gain * u] + [c * s for c, s in zip(scale, state)]
        while len(terms) > 1:
            terms = [a + b for a, b in zip(terms[::2], terms[1::2])] + (
                [terms[-1]] if len(terms) % 2 else []
            )
        conv_sc[rows, :] = terms[0]
        return state

    for lo, hi, before, reaches, ends, steps in spans(lens_ref, count, tok):

        @pl.when(hi > lo)
        def _():
            @pl.when(before)
            def _():
                spread(in_ref[...], state_sc, sub)

            @pl.when(jnp.logical_not(before))
            def _():
                state_sc[...] = jnp.zeros_like(state_sc)

            state = tuple(state_sc[p * sub : (p + 1) * sub, :] for p in range(poles))
            walk(lo, hi, step, state)

    def gate(i, _):
        start = pl.multiple_of(i * chunk, chunk)
        rows = pl.ds(start, chunk)
        for j in range(sub):
            lanes = slice(j * LANES, (j + 1) * LANES)
            conv = conv_sc[pl.ds(start * sub + j, chunk, stride=sub), :]
            out_ref[rows, lanes] = (q_ref[rows, lanes].astype(F32) * conv).astype(out_ref.dtype)
        return 0

    lax.fori_loop(0, tok // chunk, gate, 0)


def shards(q_feat, k_feat, v_feat, pole_rate, residue, skip_gain, lengths, owners):
    tok, channels = q_feat.shape
    poles, count = pole_rate.shape[0], lengths.shape[0]
    slots = lax.axis_size("ctx")
    sub = min(ROWS, channels // LANES)
    width = sub * LANES
    tiles = channels // width
    sizes = dict(tok=tok, sub=sub, poles=poles, count=count, chunk=16)
    feat = pl.BlockSpec((tok, width), lambda i, *_: (0, i))
    pole = pl.BlockSpec((poles, width), lambda i, *_: (0, i))
    slot = pl.BlockSpec((slots, poles, width), lambda i, *_: (0, 0, i))
    flat = pl.BlockSpec((tok * sub, LANES), lambda i, *_: (i, 0))
    small = pltpu.VMEM((poles * sub, LANES), F32)
    elems = tok * channels
    mixed, end, span, base, coef = pl.pallas_call(
        functools.partial(ends_kernel, **sizes),
        grid_spec=pltpu.PrefetchScalarGridSpec(
            num_scalar_prefetch=2,
            grid=(tiles,),
            in_specs=[feat, feat, pole],
            out_specs=[flat, pole, pole, slot, slot],
            scratch_shapes=[small, small],
        ),
        out_shape=[
            jax.ShapeDtypeStruct((tiles * tok * sub, LANES), F32),
            jax.ShapeDtypeStruct((poles, channels), F32),
            jax.ShapeDtypeStruct((poles, channels), F32),
            jax.ShapeDtypeStruct((slots, poles, channels), F32),
            jax.ShapeDtypeStruct((slots, poles, channels), F32),
        ],
        cost_estimate=pl.CostEstimate(
            flops=2 * poles * elems, bytes_accessed=8 * elems, transcendentals=0
        ),
        name="ends",
    )(lengths, owners, k_feat, v_feat, pole_rate)

    longest = tok * slots // 2
    hops = min((longest - 2) // tok + 1, slots - 1)
    parts = max(1, min(4, channels // LANES))
    dma = pltpu.SemaphoreType.DMA
    incoming, slotted = pl.pallas_call(
        functools.partial(relay_kernel, hops=hops, parts=parts),
        in_specs=[pl.BlockSpec(memory_space=pltpu.VMEM)] * 4,
        out_specs=[pl.BlockSpec(memory_space=pltpu.VMEM)] * 2,
        out_shape=[
            jax.ShapeDtypeStruct((poles, channels), F32),
            jax.ShapeDtypeStruct((slots, poles, channels), F32),
        ],
        scratch_shapes=[
            pltpu.VMEM((hops, poles, channels), F32),
            pltpu.VMEM((max(hops - 1, 1), poles, channels), F32),
            dma((hops, parts)), dma((hops, parts)),
        ],
        compiler_params=pltpu.CompilerParams(collective_id=0, has_side_effects=True),
        name="relay",
    )(end, span, base, coef)

    received = lax.all_to_all(
        slotted.reshape(slots, 1, poles, channels), "ctx", split_axis=0, concat_axis=0, tiled=True
    )
    decode_state = jnp.sum(received, axis=0)

    mixed_out = pl.pallas_call(
        functools.partial(conv_kernel, **sizes),
        grid_spec=pltpu.PrefetchScalarGridSpec(
            num_scalar_prefetch=1,
            grid=(tiles,),
            in_specs=[
                flat, feat, pole, pole, pl.BlockSpec((1, width), lambda i, *_: (0, i)), pole
            ],
            out_specs=feat,
            scratch_shapes=[
                small, small, small, pltpu.VMEM((sub, LANES), F32),
                pltpu.VMEM((tok * sub, LANES), F32),
            ],
        ),
        out_shape=jax.ShapeDtypeStruct((tok, channels), q_feat.dtype),
        cost_estimate=pl.CostEstimate(
            flops=8 * poles * elems, bytes_accessed=8 * elems, transcendentals=0
        ),
        name="conv",
    )(lengths, mixed, q_feat, pole_rate, residue, skip_gain[None, :], incoming)
    return mixed_out, decode_state


def solution(mesh):
    tokens = P(("groups", "ctx"), "chan")
    return jax.shard_map(
        shards,
        mesh=mesh,
        in_specs=(
            tokens, tokens, tokens, P(None, "chan"), P(None, "chan"), P("chan"),
            P("groups"), P("groups"),
        ),
        out_specs=(tokens, P(("groups", "ctx"), None, "chan")),
        check_vma=False,
    )
```

```python
import functools

import jax
import jax.numpy as jnp
from jax import lax
from jax.experimental import pallas as pl
from jax.experimental.pallas import tpu as pltpu
from jax.sharding import PartitionSpec as P

F32 = jnp.float32
LANES = 128
ROWS = 8
UNROLL = 8


def spans(lens_ref, count, tok):
    first = lax.axis_index("ctx") * tok
    offset = jnp.int32(0)
    found = []
    for r in range(count):
        size = lens_ref[r]
        end = offset + size
        lo = jnp.clip(offset - first, 0, tok)
        hi = jnp.clip(end - first, 0, tok)
        found.append((lo, hi, offset < first, end > first, end <= first + tok, end - first))
        offset = end
    return found


def spread(value, dst_ref, sub, base=0):
    for i in range(value.shape[0] // ROWS):
        for j in range(sub):
            dst_ref[pl.ds(base + i * ROWS * sub + j, ROWS, stride=sub), :] = value[
                i * ROWS : (i + 1) * ROWS, j * LANES : (j + 1) * LANES
            ]


def unspread(src_ref, dst_ref, count, sub):
    for i in range(count // ROWS):
        for j in range(sub):
            dst_ref[i * ROWS : (i + 1) * ROWS, j * LANES : (j + 1) * LANES] = src_ref[
                pl.ds(i * ROWS * sub + j, ROWS, stride=sub), :
            ]


def walk(lo, hi, step, state):
    groups = (hi - lo) // UNROLL

    def many(i, state):
        start = lo + i * UNROLL
        for k in range(UNROLL):
            state = step(start + k, state)
        return state

    state = lax.fori_loop(0, groups, many, state)
    return lax.fori_loop(lo + groups * UNROLL, hi, step, state)


def ends_kernel(
    lens_ref, own_ref, k_ref, v_ref, rate_ref, u_ref, end_ref, span_ref, base_ref, coef_ref,
    decay_sc, state_sc, *, tok, sub, poles, count, chunk,
):
    rate = rate_ref[...]
    spread(jnp.exp(-rate), decay_sc, sub)

    def mix(i, _):
        start = pl.multiple_of(i * chunk, chunk)
        u = k_ref[pl.ds(start, chunk), :].astype(F32) * v_ref[pl.ds(start, chunk), :].astype(F32)
        spread(u, u_ref, sub, start * sub)
        return 0

    lax.fori_loop(0, tok // chunk, mix, 0)
    decay = [decay_sc[p * sub : (p + 1) * sub, :] for p in range(poles)]

    def step(t, state):
        u = u_ref[pl.ds(pl.multiple_of(t * sub, sub), sub), :]
        return tuple(d * s + u for d, s in zip(decay, state))

    base_ref[...] = jnp.zeros_like(base_ref)
    coef_ref[...] = jnp.zeros_like(coef_ref)
    span_ref[...] = jnp.zeros_like(span_ref)
    zero = tuple(jnp.zeros((sub, LANES), F32) for _ in range(poles))
    for r, (lo, hi, before, reaches, ends, steps) in enumerate(spans(lens_ref, count, tok)):

        @pl.when(hi > lo)
        def _():
            state = walk(lo, hi, step, zero)
            for p in range(poles):
                state_sc[p * sub : (p + 1) * sub, :] = state[p]

            @pl.when(hi == tok)
            def _():
                unspread(state_sc, end_ref, poles, sub)

            @pl.when(ends)
            def _():
                unspread(state_sc, base_ref.at[own_ref[r]], poles, sub)

            @pl.when(before & ends)
            def _():
                coef_ref[own_ref[r]] = jnp.exp(rate * -steps.astype(F32))

            @pl.when(before & (hi == tok))
            def _():
                span_ref[...] = jnp.exp(rate * -float(tok))


def conv_kernel(
    lens_ref, end_ref, span_ref, base_ref, coef_ref, rate_ref, res_ref, gain_ref, u_hbm, q_hbm,
    out_hbm, got_ref,
    arrived, passed, slotted, landed, decay_sc, res_sc, state_sc, gain_sc, conv_sc,
    u_ref, q_ref, out_ref, sent_sem, come_sem, give_sem, take_sem, load_sem, store_sem,
    *, hops, parts, tok, sub, poles, count, chunk, tiles,
):
    slots, _, channels = base_ref.shape
    width = channels // parts
    wide = sub * LANES
    rows_in = tok * sub
    me = lax.axis_index("ctx")
    barrier = pltpu.get_barrier_semaphore()
    peers = [lax.rem(me + j, slots) for j in range(1, slots)]
    for peer in peers:
        pl.semaphore_signal(
            barrier, inc=1, device_id={"ctx": peer}, device_id_type=pl.DeviceIdType.MESH
        )
    loads = []
    for i in range(tiles):
        flat, cols = pl.ds(i * rows_in, rows_in), pl.ds(i * wide, wide)
        loads.append(
            (
                pltpu.make_async_copy(u_hbm.at[flat, :], u_ref.at[flat, :], load_sem.at[i, 0]),
                pltpu.make_async_copy(q_hbm.at[:, cols], q_ref.at[:, cols], load_sem.at[i, 1]),
            )
        )
        loads[i][0].start()
        loads[i][1].start()
    pl.semaphore_wait(barrier, slots - 1)

    def lanes(part):
        return pl.ds(part * width, width)

    def pass_on(hop, part):
        source = end_ref if hop == 0 else passed.at[hop - 1]
        return pltpu.make_async_remote_copy(
            src_ref=source.at[:, lanes(part)],
            dst_ref=arrived.at[hop, :, lanes(part)],
            send_sem=sent_sem.at[hop, part],
            recv_sem=come_sem.at[hop, part],
            device_id={"ctx": lax.rem(me + 1, slots)},
            device_id_type=pl.DeviceIdType.MESH,
        )

    def give(j, part):
        return pltpu.make_async_remote_copy(
            src_ref=slotted.at[j - 1, :, lanes(part)],
            dst_ref=landed.at[j - 1, :, lanes(part)],
            send_sem=give_sem.at[j - 1, part],
            recv_sem=take_sem.at[j - 1, part],
            device_id={"ctx": peers[j - 1]},
            device_id_type=pl.DeviceIdType.MESH,
        )

    def arrive(hop, part):
        @pl.when(me > 0)
        def _():
            pass_on(hop, part).wait_recv()

    def hop_on(hop, part):
        if hop:
            arrive(hop - 1, part)
            at = lanes(part)
            passed[hop - 1, :, at] = span_ref[:, at] * arrived[hop - 1, :, at] + end_ref[:, at]

        @pl.when(me < slots - 1)
        def _():
            pass_on(hop, part).start()

    def finish(part):
        arrive(hops - 1, part)
        at = lanes(part)
        incoming = arrived[hops - 1, :, at]
        for j in range(1, slots):
            slotted[j - 1, :, at] = (
                base_ref[peers[j - 1], :, at] + coef_ref[peers[j - 1], :, at] * incoming
            )
            give(j, part).start()
        got_ref[0, :, at] = base_ref[me, :, at] + coef_ref[me, :, at] * incoming

    @pl.when(me == 0)
    def _():
        arrived[...] = jnp.zeros_like(arrived)

    for hop in range(hops):
        for part in range(parts):
            hop_on(hop, part)

    first = me * tok
    offset = jnp.int32(0)
    starts = []
    for r in range(count):
        starts.append(offset - first)
        offset = offset + lens_ref[r]

    def conv(i, begin, stop):
        scale = [res_sc[p] for p in range(poles)]
        gain = gain_sc[...]

        def many(n, state):
            for k in range(UNROLL):
                t = n * UNROLL + k
                keep = jnp.int32(1)
                for at in starts:
                    keep = keep - (t == at).astype(jnp.int32)
                pick = jnp.maximum(keep, 0) * poles
                rows = pl.ds(pl.multiple_of(t * sub, sub), sub)
                u = u_ref[pl.ds(pl.multiple_of(i * rows_in + t * sub, sub), sub), :]
                state = tuple(decay_sc[pick + p] * s + u for p, s in enumerate(state))
                terms = [gain * u] + [c * s for c, s in zip(scale, state)]
                while len(terms) > 1:
                    terms = [a + b for a, b in zip(terms[::2], terms[1::2])] + (
                        [terms[-1]] if len(terms) % 2 else []
                    )
                conv_sc[rows, :] = terms[0]
            return state

        state = tuple(state_sc[p] for p in range(poles))
        state = lax.fori_loop(begin // UNROLL, stop // UNROLL, many, state)
        for p in range(poles):
            state_sc[p] = state[p]

    def scatter(value, ref, base):
        for p in range(poles):
            for j in range(sub):
                ref[base + p, j : j + 1, :] = value[p : p + 1, j * LANES : (j + 1) * LANES]

    stores = []
    per_tile = parts // tiles
    for i in range(tiles):
        cols = slice(i * wide, (i + 1) * wide)
        rate = rate_ref[:, cols]
        decay_sc[0:poles] = jnp.zeros((poles, sub, LANES), F32)
        scatter(jnp.exp(-rate), decay_sc, poles)
        scatter(res_ref[:, cols] * jnp.sqrt(1.0 - jnp.exp(-2.0 * rate)), res_sc, 0)
        for j in range(sub):
            at = i * wide + j * LANES
            gain_sc[j : j + 1, :] = gain_ref[0:1, at : at + LANES]
        if i == 0:
            for part in range(per_tile):
                finish(part)
        scatter(arrived[hops - 1, :, cols], state_sc, 0)
        loads[i][0].wait()
        if i == 0 and tiles > 1:
            conv(i, 0, tok // 4)
            for part in range(per_tile, parts):
                finish(part)
            conv(i, tok // 4, tok)
        else:
            conv(i, 0, tok)
        loads[i][1].wait()

        def gate(n, _):
            start = pl.multiple_of(n * chunk, chunk)
            rows = pl.ds(start, chunk)
            for j in range(sub):
                at = slice(i * wide + j * LANES, i * wide + (j + 1) * LANES)
                value = conv_sc[pl.ds(start * sub + j, chunk, stride=sub), :]
                out_ref[rows, at] = (q_ref[rows, at].astype(F32) * value).astype(out_ref.dtype)
            return 0

        lax.fori_loop(0, tok // chunk, gate, 0)
        stores.append(
            pltpu.make_async_copy(
                out_ref.at[:, pl.ds(i * wide, wide)], out_hbm.at[:, pl.ds(i * wide, wide)],
                store_sem.at[i],
            )
        )
        stores[i].start()

    for part in range(parts):
        at = lanes(part)
        for j in range(1, slots):
            give(j, part).wait_recv()
        total = got_ref[0, :, at]
        for j in range(1, slots):
            total += landed[j - 1, :, at]
        got_ref[0, :, at] = total
    for part in range(parts):
        for j in range(1, slots):
            give(j, part).wait_send()

    @pl.when(me < slots - 1)
    def _():
        for hop in range(hops):
            for part in range(parts):
                pass_on(hop, part).wait_send()

    for copy in stores:
        copy.wait()


def shards(q_feat, k_feat, v_feat, pole_rate, residue, skip_gain, lengths, owners):
    tok, channels = q_feat.shape
    poles, count = pole_rate.shape[0], lengths.shape[0]
    slots = lax.axis_size("ctx")
    sub = min(ROWS, channels // LANES)
    width = sub * LANES
    tiles = channels // width
    sizes = dict(tok=tok, sub=sub, poles=poles, count=count, chunk=16)
    feat = pl.BlockSpec((tok, width), lambda i, *_: (0, i))
    pole = pl.BlockSpec((poles, width), lambda i, *_: (0, i))
    slot = pl.BlockSpec((slots, poles, width), lambda i, *_: (0, 0, i))
    flat = pl.BlockSpec((tok * sub, LANES), lambda i, *_: (i, 0))
    small = pltpu.VMEM((poles * sub, LANES), F32)
    elems = tok * channels
    mixed, end, span, base, coef = pl.pallas_call(
        functools.partial(ends_kernel, **sizes),
        grid_spec=pltpu.PrefetchScalarGridSpec(
            num_scalar_prefetch=2,
            grid=(tiles,),
            in_specs=[feat, feat, pole],
            out_specs=[flat, pole, pole, slot, slot],
            scratch_shapes=[small, small],
        ),
        out_shape=[
            jax.ShapeDtypeStruct((tiles * tok * sub, LANES), F32),
            jax.ShapeDtypeStruct((poles, channels), F32),
            jax.ShapeDtypeStruct((poles, channels), F32),
            jax.ShapeDtypeStruct((slots, poles, channels), F32),
            jax.ShapeDtypeStruct((slots, poles, channels), F32),
        ],
        cost_estimate=pl.CostEstimate(
            flops=2 * poles * elems, bytes_accessed=8 * elems, transcendentals=0
        ),
        name="ends",
    )(lengths, owners, k_feat, v_feat, pole_rate)

    longest = tok * slots // 2
    hops = min((longest - 2) // tok + 1, slots - 1)
    parts = max(tiles, min(4, channels // LANES))
    dma = pltpu.SemaphoreType.DMA
    vmem, hbm = pl.BlockSpec(memory_space=pltpu.VMEM), pl.BlockSpec(memory_space=pl.ANY)
    mixed_out, decode_state = pl.pallas_call(
        functools.partial(conv_kernel, hops=hops, parts=parts, tiles=tiles, **sizes),
        in_specs=[pl.BlockSpec(memory_space=pltpu.SMEM)] + [vmem] * 7 + [hbm] * 2,
        out_specs=[hbm, vmem],
        out_shape=[
            jax.ShapeDtypeStruct((tok, channels), q_feat.dtype),
            jax.ShapeDtypeStruct((1, poles, channels), F32),
        ],
        scratch_shapes=[
            pltpu.VMEM((hops, poles, channels), F32),
            pltpu.VMEM((max(hops - 1, 1), poles, channels), F32),
            pltpu.VMEM((slots - 1, poles, channels), F32),
            pltpu.VMEM((slots - 1, poles, channels), F32),
            pltpu.VMEM((2 * poles, sub, LANES), F32),
            pltpu.VMEM((poles, sub, LANES), F32),
            pltpu.VMEM((poles, sub, LANES), F32),
            pltpu.VMEM((sub, LANES), F32),
            pltpu.VMEM((tok * sub, LANES), F32),
            pltpu.VMEM((tiles * tok * sub, LANES), F32),
            pltpu.VMEM((tok, channels), q_feat.dtype),
            pltpu.VMEM((tok, channels), q_feat.dtype),
            dma((hops, parts)), dma((hops, parts)),
            dma((slots - 1, parts)), dma((slots - 1, parts)),
            dma((tiles, 2)), dma((tiles,)),
        ],
        compiler_params=pltpu.CompilerParams(collective_id=0, has_side_effects=True),
        name="conv",
    )(
        lengths, end, span, base, coef, pole_rate, residue, skip_gain[None, :], mixed, q_feat
    )
    return mixed_out, decode_state


def solution(mesh):
    tokens = P(("groups", "ctx"), "chan")
    return jax.shard_map(
        shards,
        mesh=mesh,
        in_specs=(
            tokens, tokens, tokens, P(None, "chan"), P(None, "chan"), P("chan"),
            P("groups"), P("groups"),
        ),
        out_specs=(tokens, P(("groups", "ctx"), None, "chan")),
        check_vma=False,
    )
```

```python
import functools

import jax
import jax.numpy as jnp
from jax import lax
from jax.experimental import pallas as pl
from jax.experimental.pallas import tpu as pltpu
from jax.sharding import PartitionSpec as P

F32 = jnp.float32
LANES = 128
ROWS = 8
UNROLL = 8


def spans(lens_ref, count, tok):
    first = lax.axis_index("ctx") * tok
    offset = jnp.int32(0)
    found = []
    for r in range(count):
        size = lens_ref[r]
        end = offset + size
        lo = jnp.clip(offset - first, 0, tok)
        hi = jnp.clip(end - first, 0, tok)
        found.append((lo, hi, offset < first, end > first, end <= first + tok, end - first))
        offset = end
    return found


def spread(value, dst_ref, sub, base=0):
    for i in range(value.shape[0] // ROWS):
        for j in range(sub):
            dst_ref[pl.ds(base + i * ROWS * sub + j, ROWS, stride=sub), :] = value[
                i * ROWS : (i + 1) * ROWS, j * LANES : (j + 1) * LANES
            ]


def unspread(src_ref, dst_ref, count, sub):
    for i in range(count // ROWS):
        for j in range(sub):
            dst_ref[i * ROWS : (i + 1) * ROWS, j * LANES : (j + 1) * LANES] = src_ref[
                pl.ds(i * ROWS * sub + j, ROWS, stride=sub), :
            ]


def walk(lo, hi, step, state):
    groups = (hi - lo) // UNROLL

    def many(i, state):
        start = lo + i * UNROLL
        for k in range(UNROLL):
            state = step(start + k, state)
        return state

    state = lax.fori_loop(0, groups, many, state)
    return lax.fori_loop(lo + groups * UNROLL, hi, step, state)


def ends_kernel(
    lens_ref, own_ref, k_ref, v_ref, rate_ref, u_ref, end_ref, span_ref, base_ref, coef_ref,
    decay_sc, state_sc, *, tok, sub, poles, count, chunk,
):
    rate = rate_ref[...]
    spread(jnp.exp(-rate), decay_sc, sub)

    def mix(i, _):
        start = pl.multiple_of(i * chunk, chunk)
        u = k_ref[pl.ds(start, chunk), :].astype(F32) * v_ref[pl.ds(start, chunk), :].astype(F32)
        spread(u, u_ref, sub, start * sub)
        return 0

    lax.fori_loop(0, tok // chunk, mix, 0)
    decay = [decay_sc[p * sub : (p + 1) * sub, :] for p in range(poles)]

    def step(t, state):
        u = u_ref[pl.ds(pl.multiple_of(t * sub, sub), sub), :]
        return tuple(d * s + u for d, s in zip(decay, state))

    base_ref[...] = jnp.zeros_like(base_ref)
    coef_ref[...] = jnp.zeros_like(coef_ref)
    span_ref[...] = jnp.zeros_like(span_ref)
    zero = tuple(jnp.zeros((sub, LANES), F32) for _ in range(poles))
    for r, (lo, hi, before, reaches, ends, steps) in enumerate(spans(lens_ref, count, tok)):

        @pl.when(hi > lo)
        def _():
            state = walk(lo, hi, step, zero)
            for p in range(poles):
                state_sc[p * sub : (p + 1) * sub, :] = state[p]

            @pl.when(hi == tok)
            def _():
                unspread(state_sc, end_ref, poles, sub)

            @pl.when(ends)
            def _():
                unspread(state_sc, base_ref.at[own_ref[r]], poles, sub)

            @pl.when(before & ends)
            def _():
                coef_ref[own_ref[r]] = jnp.exp(rate * -steps.astype(F32))

            @pl.when(before & (hi == tok))
            def _():
                span_ref[...] = jnp.exp(rate * -float(tok))


def conv_kernel(
    lens_ref, end_ref, span_ref, base_ref, coef_ref, rate_ref, res_ref, gain_ref, u_hbm,
    conv_hbm, got_ref,
    arrived, passed, slotted, landed, decay_sc, res_sc, state_sc, gain_sc, conv_sc,
    u_ref, sent_sem, come_sem, give_sem, take_sem, load_sem, store_sem,
    *, hops, parts, tok, sub, poles, count, tiles,
):
    slots, _, channels = base_ref.shape
    width = channels // parts
    wide = sub * LANES
    rows_in = tok * sub
    me = lax.axis_index("ctx")
    barrier = pltpu.get_barrier_semaphore()
    peers = [lax.rem(me + j, slots) for j in range(1, slots)]
    for peer in peers:
        pl.semaphore_signal(
            barrier, inc=1, device_id={"ctx": peer}, device_id_type=pl.DeviceIdType.MESH
        )
    loads = []
    for i in range(tiles):
        flat = pl.ds(i * rows_in, rows_in)
        loads.append(
            pltpu.make_async_copy(u_hbm.at[flat, :], u_ref.at[flat, :], load_sem.at[i])
        )
        loads[i].start()
    pl.semaphore_wait(barrier, slots - 1)

    def lanes(part):
        return pl.ds(part * width, width)

    def pass_on(hop, part):
        source = end_ref if hop == 0 else passed.at[hop - 1]
        return pltpu.make_async_remote_copy(
            src_ref=source.at[:, lanes(part)],
            dst_ref=arrived.at[hop, :, lanes(part)],
            send_sem=sent_sem.at[hop, part],
            recv_sem=come_sem.at[hop, part],
            device_id={"ctx": lax.rem(me + 1, slots)},
            device_id_type=pl.DeviceIdType.MESH,
        )

    def give(j, part):
        return pltpu.make_async_remote_copy(
            src_ref=slotted.at[j - 1, :, lanes(part)],
            dst_ref=landed.at[j - 1, :, lanes(part)],
            send_sem=give_sem.at[j - 1, part],
            recv_sem=take_sem.at[j - 1, part],
            device_id={"ctx": peers[j - 1]},
            device_id_type=pl.DeviceIdType.MESH,
        )

    def arrive(hop, part):
        @pl.when(me > 0)
        def _():
            pass_on(hop, part).wait_recv()

    def hop_on(hop, part):
        if hop:
            arrive(hop - 1, part)
            at = lanes(part)
            passed[hop - 1, :, at] = span_ref[:, at] * arrived[hop - 1, :, at] + end_ref[:, at]

        @pl.when(me < slots - 1)
        def _():
            pass_on(hop, part).start()

    def finish(part):
        arrive(hops - 1, part)
        at = lanes(part)
        incoming = arrived[hops - 1, :, at]
        for j in range(1, slots):
            slotted[j - 1, :, at] = (
                base_ref[peers[j - 1], :, at] + coef_ref[peers[j - 1], :, at] * incoming
            )
            give(j, part).start()
        got_ref[0, :, at] = base_ref[me, :, at] + coef_ref[me, :, at] * incoming

    @pl.when(me == 0)
    def _():
        arrived[...] = jnp.zeros_like(arrived)

    for hop in range(hops):
        for part in range(parts):
            hop_on(hop, part)

    first = me * tok
    offset = jnp.int32(0)
    starts = []
    for r in range(count):
        starts.append(offset - first)
        offset = offset + lens_ref[r]

    def conv(i, begin, stop):
        scale = [res_sc[p] for p in range(poles)]
        gain = gain_sc[...]

        def many(n, state):
            for k in range(UNROLL):
                t = n * UNROLL + k
                keep = jnp.int32(1)
                for at in starts:
                    keep = keep - (t == at).astype(jnp.int32)
                pick = jnp.maximum(keep, 0) * poles
                rows = pl.ds(pl.multiple_of(i * rows_in + t * sub, sub), sub)
                u = u_ref[rows, :]
                state = tuple(decay_sc[pick + p] * s + u for p, s in enumerate(state))
                terms = [gain * u] + [c * s for c, s in zip(scale, state)]
                while len(terms) > 1:
                    terms = [a + b for a, b in zip(terms[::2], terms[1::2])] + (
                        [terms[-1]] if len(terms) % 2 else []
                    )
                conv_sc[rows, :] = terms[0]
            return state

        state = tuple(state_sc[p] for p in range(poles))
        state = lax.fori_loop(begin // UNROLL, stop // UNROLL, many, state)
        for p in range(poles):
            state_sc[p] = state[p]
        rows = pl.ds(i * rows_in + begin * sub, (stop - begin) * sub)
        stores.append(
            pltpu.make_async_copy(
                conv_sc.at[rows, :], conv_hbm.at[rows, :], store_sem.at[len(stores)]
            )
        )
        stores[-1].start()

    def scatter(value, ref, base):
        for p in range(poles):
            for j in range(sub):
                ref[base + p, j : j + 1, :] = value[p : p + 1, j * LANES : (j + 1) * LANES]

    stores = []
    per_tile = parts // tiles
    for i in range(tiles):
        cols = slice(i * wide, (i + 1) * wide)
        rate = rate_ref[:, cols]
        decay_sc[0:poles] = jnp.zeros((poles, sub, LANES), F32)
        scatter(jnp.exp(-rate), decay_sc, poles)
        scatter(res_ref[:, cols] * jnp.sqrt(1.0 - jnp.exp(-2.0 * rate)), res_sc, 0)
        for j in range(sub):
            at = i * wide + j * LANES
            gain_sc[j : j + 1, :] = gain_ref[0:1, at : at + LANES]
        if i == 0:
            for part in range(per_tile):
                finish(part)
        scatter(arrived[hops - 1, :, cols], state_sc, 0)
        loads[i].wait()
        cut = tok // 4 if i == 0 else tok - tok // 4
        conv(i, 0, cut)
        if i == 0:
            for part in range(per_tile, parts):
                finish(part)
        conv(i, cut, tok)

    for part in range(parts):
        at = lanes(part)
        for j in range(1, slots):
            give(j, part).wait_recv()
        total = got_ref[0, :, at]
        for j in range(1, slots):
            total += landed[j - 1, :, at]
        got_ref[0, :, at] = total
    for part in range(parts):
        for j in range(1, slots):
            give(j, part).wait_send()

    @pl.when(me < slots - 1)
    def _():
        for hop in range(hops):
            for part in range(parts):
                pass_on(hop, part).wait_send()

    for copy in stores:
        copy.wait()


def gate_kernel(conv_ref, q_ref, got_ref, out_ref, kept_ref, *, sub, chunk):
    kept_ref[...] = got_ref[...]

    def gate(n, _):
        start = pl.multiple_of(n * chunk, chunk)
        rows = pl.ds(start, chunk)
        for j in range(sub):
            at = slice(j * LANES, (j + 1) * LANES)
            value = conv_ref[pl.ds(start * sub + j, chunk, stride=sub), :]
            out_ref[rows, at] = (q_ref[rows, at].astype(F32) * value).astype(out_ref.dtype)
        return 0

    lax.fori_loop(0, q_ref.shape[0] // chunk, gate, 0)


def shards(q_feat, k_feat, v_feat, pole_rate, residue, skip_gain, lengths, owners):
    tok, channels = q_feat.shape
    poles, count = pole_rate.shape[0], lengths.shape[0]
    slots = lax.axis_size("ctx")
    sub = min(ROWS, channels // LANES)
    width = sub * LANES
    tiles = channels // width
    shape = dict(tok=tok, sub=sub, poles=poles, count=count)
    sizes = dict(shape, chunk=16)
    feat = pl.BlockSpec((tok, width), lambda i, *_: (0, i))
    pole = pl.BlockSpec((poles, width), lambda i, *_: (0, i))
    slot = pl.BlockSpec((slots, poles, width), lambda i, *_: (0, 0, i))
    flat = pl.BlockSpec((tok * sub, LANES), lambda i, *_: (i, 0))
    small = pltpu.VMEM((poles * sub, LANES), F32)
    elems = tok * channels
    mixed, end, span, base, coef = pl.pallas_call(
        functools.partial(ends_kernel, **sizes),
        grid_spec=pltpu.PrefetchScalarGridSpec(
            num_scalar_prefetch=2,
            grid=(tiles,),
            in_specs=[feat, feat, pole],
            out_specs=[flat, pole, pole, slot, slot],
            scratch_shapes=[small, small],
        ),
        out_shape=[
            jax.ShapeDtypeStruct((tiles * tok * sub, LANES), F32),
            jax.ShapeDtypeStruct((poles, channels), F32),
            jax.ShapeDtypeStruct((poles, channels), F32),
            jax.ShapeDtypeStruct((slots, poles, channels), F32),
            jax.ShapeDtypeStruct((slots, poles, channels), F32),
        ],
        cost_estimate=pl.CostEstimate(
            flops=2 * poles * elems, bytes_accessed=8 * elems, transcendentals=0
        ),
        name="ends",
    )(lengths, owners, k_feat, v_feat, pole_rate)

    longest = tok * slots // 2
    hops = min((longest - 2) // tok + 1, slots - 1)
    parts = max(tiles, min(4, channels // LANES))
    dma = pltpu.SemaphoreType.DMA
    vmem, hbm = pl.BlockSpec(memory_space=pltpu.VMEM), pl.BlockSpec(memory_space=pl.ANY)
    conv, got = pl.pallas_call(
        functools.partial(conv_kernel, hops=hops, parts=parts, tiles=tiles, **shape),
        in_specs=[pl.BlockSpec(memory_space=pltpu.SMEM)] + [vmem] * 7 + [hbm],
        out_specs=[hbm, vmem],
        out_shape=[
            jax.ShapeDtypeStruct((tiles * tok * sub, LANES), F32),
            jax.ShapeDtypeStruct((1, poles, channels), F32),
        ],
        scratch_shapes=[
            pltpu.VMEM((hops, poles, channels), F32),
            pltpu.VMEM((max(hops - 1, 1), poles, channels), F32),
            pltpu.VMEM((slots - 1, poles, channels), F32),
            pltpu.VMEM((slots - 1, poles, channels), F32),
            pltpu.VMEM((2 * poles, sub, LANES), F32),
            pltpu.VMEM((poles, sub, LANES), F32),
            pltpu.VMEM((poles, sub, LANES), F32),
            pltpu.VMEM((sub, LANES), F32),
            pltpu.VMEM((tiles * tok * sub, LANES), F32),
            pltpu.VMEM((tiles * tok * sub, LANES), F32),
            dma((hops, parts)), dma((hops, parts)),
            dma((slots - 1, parts)), dma((slots - 1, parts)),
            dma((tiles,)), dma((2 * tiles,)),
        ],
        compiler_params=pltpu.CompilerParams(collective_id=0, has_side_effects=True),
        name="conv",
    )(
        lengths, end, span, base, coef, pole_rate, residue, skip_gain[None, :], mixed
    )
    cuts = 4
    rows = tok // cuts
    block = pl.BlockSpec((rows, width), lambda i, n: (n, i))
    whole = pl.BlockSpec((1, poles, channels), lambda i, n: (0, 0, 0))
    mixed_out, decode_state = pl.pallas_call(
        functools.partial(gate_kernel, sub=sub, chunk=16),
        grid=(tiles, cuts),
        in_specs=[
            pl.BlockSpec((rows * sub, LANES), lambda i, n: (i * cuts + n, 0)), block, whole
        ],
        out_specs=[block, whole],
        out_shape=[
            jax.ShapeDtypeStruct((tok, channels), q_feat.dtype),
            jax.ShapeDtypeStruct((1, poles, channels), F32),
        ],
        name="gate",
    )(conv, q_feat, got)
    return mixed_out, decode_state


def solution(mesh):
    tokens = P(("groups", "ctx"), "chan")
    return jax.shard_map(
        shards,
        mesh=mesh,
        in_specs=(
            tokens, tokens, tokens, P(None, "chan"), P(None, "chan"), P("chan"),
            P("groups"), P("groups"),
        ),
        out_specs=(tokens, P(("groups", "ctx"), None, "chan")),
        check_vma=False,
    )
```

```python
import functools

import jax
import jax.numpy as jnp
from jax import lax
from jax.experimental import pallas as pl
from jax.experimental.pallas import tpu as pltpu
from jax.sharding import PartitionSpec as P

F32 = jnp.float32
LANES = 128
ROWS = 8
UNROLL = 8


def spans(lens_ref, count, tok):
    first = lax.axis_index("ctx") * tok
    offset = jnp.int32(0)
    found = []
    for r in range(count):
        size = lens_ref[r]
        end = offset + size
        lo = jnp.clip(offset - first, 0, tok)
        hi = jnp.clip(end - first, 0, tok)
        found.append((lo, hi, offset < first, end > first, end <= first + tok, end - first))
        offset = end
    return found


def spread(value, dst_ref, sub, base=0):
    for i in range(value.shape[0] // ROWS):
        for j in range(sub):
            dst_ref[pl.ds(base + i * ROWS * sub + j, ROWS, stride=sub), :] = value[
                i * ROWS : (i + 1) * ROWS, j * LANES : (j + 1) * LANES
            ]


def unspread(src_ref, dst_ref, count, sub):
    for i in range(count // ROWS):
        for j in range(sub):
            dst_ref[i * ROWS : (i + 1) * ROWS, j * LANES : (j + 1) * LANES] = src_ref[
                pl.ds(i * ROWS * sub + j, ROWS, stride=sub), :
            ]


def walk(lo, hi, step, state):
    groups = (hi - lo) // UNROLL

    def many(i, state):
        start = lo + i * UNROLL
        for k in range(UNROLL):
            state = step(start + k, state)
        return state

    state = lax.fori_loop(0, groups, many, state)
    return lax.fori_loop(lo + groups * UNROLL, hi, step, state)


def ends_kernel(
    lens_ref, own_ref, k_ref, v_ref, rate_ref, u_ref, end_ref, span_ref, base_ref, coef_ref,
    decay_sc, state_sc, *, tok, sub, poles, count, chunk,
):
    rate = rate_ref[...]
    spread(jnp.exp(-rate), decay_sc, sub)

    def mix(i, _):
        start = pl.multiple_of(i * chunk, chunk)
        u = k_ref[pl.ds(start, chunk), :].astype(F32) * v_ref[pl.ds(start, chunk), :].astype(F32)
        spread(u, u_ref, sub, start * sub)
        return 0

    lax.fori_loop(0, tok // chunk, mix, 0)
    decay = [decay_sc[p * sub : (p + 1) * sub, :] for p in range(poles)]

    def step(t, state):
        u = u_ref[pl.ds(pl.multiple_of(t * sub, sub), sub), :]
        return tuple(d * s + u for d, s in zip(decay, state))

    base_ref[...] = jnp.zeros_like(base_ref)
    coef_ref[...] = jnp.zeros_like(coef_ref)
    span_ref[...] = jnp.zeros_like(span_ref)
    zero = tuple(jnp.zeros((sub, LANES), F32) for _ in range(poles))
    for r, (lo, hi, before, reaches, ends, steps) in enumerate(spans(lens_ref, count, tok)):

        @pl.when(hi > lo)
        def _():
            state = walk(lo, hi, step, zero)
            for p in range(poles):
                state_sc[p * sub : (p + 1) * sub, :] = state[p]

            @pl.when(hi == tok)
            def _():
                unspread(state_sc, end_ref, poles, sub)

            @pl.when(ends)
            def _():
                unspread(state_sc, base_ref.at[own_ref[r]], poles, sub)

            @pl.when(before & ends)
            def _():
                coef_ref[own_ref[r]] = jnp.exp(rate * -steps.astype(F32))

            @pl.when(before & (hi == tok))
            def _():
                span_ref[...] = jnp.exp(rate * -float(tok))


def conv_kernel(
    lens_ref, end_ref, span_ref, base_ref, coef_ref, rate_ref, res_ref, gain_ref, u_hbm, q_hbm,
    out_hbm, got_ref,
    arrived, passed, slotted, landed, decay_sc, res_sc, state_sc, gain_sc, conv_sc,
    u_ref, q_ref, out_ref, sent_sem, come_sem, give_sem, take_sem, load_sem, store_sem,
    *, hops, parts, tok, sub, poles, count, chunk, tiles,
):
    slots, _, channels = base_ref.shape
    width = channels // parts
    wide = sub * LANES
    rows_in = tok * sub
    me = lax.axis_index("ctx")
    barrier = pltpu.get_barrier_semaphore()
    peers = [lax.rem(me + j, slots) for j in range(1, slots)]
    for peer in peers:
        pl.semaphore_signal(
            barrier, inc=1, device_id={"ctx": peer}, device_id_type=pl.DeviceIdType.MESH
        )
    loads = []
    for i in range(tiles):
        flat, cols = pl.ds(i * rows_in, rows_in), pl.ds(i * wide, wide)
        loads.append(
            (
                pltpu.make_async_copy(u_hbm.at[flat, :], u_ref.at[flat, :], load_sem.at[i, 0]),
                pltpu.make_async_copy(q_hbm.at[:, cols], q_ref.at[:, cols], load_sem.at[i, 1]),
            )
        )
        loads[i][0].start()
        loads[i][1].start()
    pl.semaphore_wait(barrier, slots - 1)

    def lanes(part):
        return pl.ds(part * width, width)

    def pass_on(hop, part):
        source = end_ref if hop == 0 else passed.at[hop - 1]
        return pltpu.make_async_remote_copy(
            src_ref=source.at[:, lanes(part)],
            dst_ref=arrived.at[hop, :, lanes(part)],
            send_sem=sent_sem.at[hop, part],
            recv_sem=come_sem.at[hop, part],
            device_id={"ctx": lax.rem(me + 1, slots)},
            device_id_type=pl.DeviceIdType.MESH,
        )

    def give(j, part):
        return pltpu.make_async_remote_copy(
            src_ref=slotted.at[j - 1, :, lanes(part)],
            dst_ref=landed.at[j - 1, :, lanes(part)],
            send_sem=give_sem.at[j - 1, part],
            recv_sem=take_sem.at[j - 1, part],
            device_id={"ctx": peers[j - 1]},
            device_id_type=pl.DeviceIdType.MESH,
        )

    def arrive(hop, part):
        @pl.when(me > 0)
        def _():
            pass_on(hop, part).wait_recv()

    def hop_on(hop, part):
        if hop:
            arrive(hop - 1, part)
            at = lanes(part)
            passed[hop - 1, :, at] = span_ref[:, at] * arrived[hop - 1, :, at] + end_ref[:, at]

        @pl.when(me < slots - 1)
        def _():
            pass_on(hop, part).start()

    def finish(part):
        arrive(hops - 1, part)
        at = lanes(part)
        incoming = arrived[hops - 1, :, at]
        for j in range(1, slots):
            slotted[j - 1, :, at] = (
                base_ref[peers[j - 1], :, at] + coef_ref[peers[j - 1], :, at] * incoming
            )
            give(j, part).start()
        got_ref[0, :, at] = base_ref[me, :, at] + coef_ref[me, :, at] * incoming

    @pl.when(me == 0)
    def _():
        arrived[...] = jnp.zeros_like(arrived)

    for hop in range(hops):
        for part in range(parts):
            hop_on(hop, part)

    first = me * tok
    offset = jnp.int32(0)
    starts = []
    for r in range(count):
        starts.append(offset - first)
        offset = offset + lens_ref[r]

    def conv(i, begin, stop):
        scale = [res_sc[p] for p in range(poles)]
        gain = gain_sc[...]

        def many(n, state):
            for k in range(UNROLL):
                t = n * UNROLL + k
                keep = jnp.int32(1)
                for at in starts:
                    keep = keep - (t == at).astype(jnp.int32)
                pick = jnp.maximum(keep, 0) * poles
                rows = pl.ds(pl.multiple_of(t * sub, sub), sub)
                u = u_ref[pl.ds(pl.multiple_of(i * rows_in + t * sub, sub), sub), :]
                state = tuple(decay_sc[pick + p] * s + u for p, s in enumerate(state))
                terms = [gain * u] + [c * s for c, s in zip(scale, state)]
                while len(terms) > 1:
                    terms = [a + b for a, b in zip(terms[::2], terms[1::2])] + (
                        [terms[-1]] if len(terms) % 2 else []
                    )
                conv_sc[rows, :] = terms[0]
            return state

        state = tuple(state_sc[p] for p in range(poles))
        state = lax.fori_loop(begin // UNROLL, stop // UNROLL, many, state)
        for p in range(poles):
            state_sc[p] = state[p]

    def scatter(value, ref, base):
        for p in range(poles):
            for j in range(sub):
                ref[base + p, j : j + 1, :] = value[p : p + 1, j * LANES : (j + 1) * LANES]

    stores = []
    for i in range(tiles):
        cols = slice(i * wide, (i + 1) * wide)
        rate = rate_ref[:, cols]
        decay_sc[0:poles] = jnp.zeros((poles, sub, LANES), F32)
        scatter(jnp.exp(-rate), decay_sc, poles)
        scatter(res_ref[:, cols] * jnp.sqrt(1.0 - jnp.exp(-2.0 * rate)), res_sc, 0)
        for j in range(sub):
            at = i * wide + j * LANES
            gain_sc[j : j + 1, :] = gain_ref[0:1, at : at + LANES]
        if i == 0:
            for part in range(parts):
                finish(part)
        scatter(arrived[hops - 1, :, cols], state_sc, 0)
        loads[i][0].wait()
        conv(i, 0, tok)
        loads[i][1].wait()

        def gate(n, _):
            start = pl.multiple_of(n * chunk, chunk)
            rows = pl.ds(start, chunk)
            for j in range(sub):
                at = slice(i * wide + j * LANES, i * wide + (j + 1) * LANES)
                value = conv_sc[pl.ds(start * sub + j, chunk, stride=sub), :]
                out_ref[rows, at] = (q_ref[rows, at].astype(F32) * value).astype(out_ref.dtype)
            return 0

        lax.fori_loop(0, tok // chunk, gate, 0)
        stores.append(
            pltpu.make_async_copy(
                out_ref.at[:, pl.ds(i * wide, wide)], out_hbm.at[:, pl.ds(i * wide, wide)],
                store_sem.at[i],
            )
        )
        stores[i].start()

    for part in range(parts):
        at = lanes(part)
        for j in range(1, slots):
            give(j, part).wait_recv()
        total = got_ref[0, :, at]
        for j in range(1, slots):
            total += landed[j - 1, :, at]
        got_ref[0, :, at] = total
    for part in range(parts):
        for j in range(1, slots):
            give(j, part).wait_send()

    @pl.when(me < slots - 1)
    def _():
        for hop in range(hops):
            for part in range(parts):
                pass_on(hop, part).wait_send()

    for copy in stores:
        copy.wait()


def shards(q_feat, k_feat, v_feat, pole_rate, residue, skip_gain, lengths, owners):
    tok, channels = q_feat.shape
    poles, count = pole_rate.shape[0], lengths.shape[0]
    slots = lax.axis_size("ctx")
    sub = min(ROWS, channels // LANES)
    width = sub * LANES
    tiles = channels // width
    sizes = dict(tok=tok, sub=sub, poles=poles, count=count, chunk=16)
    feat = pl.BlockSpec((tok, width), lambda i, *_: (0, i))
    pole = pl.BlockSpec((poles, width), lambda i, *_: (0, i))
    slot = pl.BlockSpec((slots, poles, width), lambda i, *_: (0, 0, i))
    flat = pl.BlockSpec((tok * sub, LANES), lambda i, *_: (i, 0))
    small = pltpu.VMEM((poles * sub, LANES), F32)
    elems = tok * channels
    mixed, end, span, base, coef = pl.pallas_call(
        functools.partial(ends_kernel, **sizes),
        grid_spec=pltpu.PrefetchScalarGridSpec(
            num_scalar_prefetch=2,
            grid=(tiles,),
            in_specs=[feat, feat, pole],
            out_specs=[flat, pole, pole, slot, slot],
            scratch_shapes=[small, small],
        ),
        out_shape=[
            jax.ShapeDtypeStruct((tiles * tok * sub, LANES), F32),
            jax.ShapeDtypeStruct((poles, channels), F32),
            jax.ShapeDtypeStruct((poles, channels), F32),
            jax.ShapeDtypeStruct((slots, poles, channels), F32),
            jax.ShapeDtypeStruct((slots, poles, channels), F32),
        ],
        cost_estimate=pl.CostEstimate(
            flops=2 * poles * elems, bytes_accessed=8 * elems, transcendentals=0
        ),
        name="ends",
    )(lengths, owners, k_feat, v_feat, pole_rate)

    longest = tok * slots // 2
    hops = min((longest - 2) // tok + 1, slots - 1)
    parts = max(tiles, min(4, channels // LANES))
    dma = pltpu.SemaphoreType.DMA
    vmem, hbm = pl.BlockSpec(memory_space=pltpu.VMEM), pl.BlockSpec(memory_space=pl.ANY)
    mixed_out, decode_state = pl.pallas_call(
        functools.partial(conv_kernel, hops=hops, parts=parts, tiles=tiles, **sizes),
        in_specs=[pl.BlockSpec(memory_space=pltpu.SMEM)] + [vmem] * 7 + [hbm] * 2,
        out_specs=[hbm, vmem],
        out_shape=[
            jax.ShapeDtypeStruct((tok, channels), q_feat.dtype),
            jax.ShapeDtypeStruct((1, poles, channels), F32),
        ],
        scratch_shapes=[
            pltpu.VMEM((hops, poles, channels), F32),
            pltpu.VMEM((max(hops - 1, 1), poles, channels), F32),
            pltpu.VMEM((slots - 1, poles, channels), F32),
            pltpu.VMEM((slots - 1, poles, channels), F32),
            pltpu.VMEM((2 * poles, sub, LANES), F32),
            pltpu.VMEM((poles, sub, LANES), F32),
            pltpu.VMEM((poles, sub, LANES), F32),
            pltpu.VMEM((sub, LANES), F32),
            pltpu.VMEM((tok * sub, LANES), F32),
            pltpu.VMEM((tiles * tok * sub, LANES), F32),
            pltpu.VMEM((tok, channels), q_feat.dtype),
            pltpu.VMEM((tok, channels), q_feat.dtype),
            dma((hops, parts)), dma((hops, parts)),
            dma((slots - 1, parts)), dma((slots - 1, parts)),
            dma((tiles, 2)), dma((tiles,)),
        ],
        compiler_params=pltpu.CompilerParams(collective_id=0, has_side_effects=True),
        name="conv",
    )(
        lengths, end, span, base, coef, pole_rate, residue, skip_gain[None, :], mixed, q_feat
    )
    return mixed_out, decode_state


def solution(mesh):
    tokens = P(("groups", "ctx"), "chan")
    return jax.shard_map(
        shards,
        mesh=mesh,
        in_specs=(
            tokens, tokens, tokens, P(None, "chan"), P(None, "chan"), P("chan"),
            P("groups"), P("groups"),
        ),
        out_specs=(tokens, P(("groups", "ctx"), None, "chan")),
        check_vma=False,
    )
```

```python
import functools

import jax
import jax.numpy as jnp
from jax import lax
from jax.experimental import pallas as pl
from jax.experimental.pallas import tpu as pltpu
from jax.sharding import PartitionSpec as P

F32 = jnp.float32
LANES = 128
ROWS = 8
UNROLL = 8
DEEP = 16


def spans(lens_ref, count, tok):
    first = lax.axis_index("ctx") * tok
    offset = jnp.int32(0)
    found = []
    for r in range(count):
        size = lens_ref[r]
        end = offset + size
        lo = jnp.clip(offset - first, 0, tok)
        hi = jnp.clip(end - first, 0, tok)
        found.append((lo, hi, offset < first, end > first, end <= first + tok, end - first))
        offset = end
    return found


def spread(value, dst_ref, sub, base=0):
    for i in range(value.shape[0] // ROWS):
        for j in range(sub):
            dst_ref[pl.ds(base + i * ROWS * sub + j, ROWS, stride=sub), :] = value[
                i * ROWS : (i + 1) * ROWS, j * LANES : (j + 1) * LANES
            ]


def unspread(src_ref, dst_ref, count, sub):
    for i in range(count // ROWS):
        for j in range(sub):
            dst_ref[i * ROWS : (i + 1) * ROWS, j * LANES : (j + 1) * LANES] = src_ref[
                pl.ds(i * ROWS * sub + j, ROWS, stride=sub), :
            ]


def walk(lo, hi, step, state):
    groups = (hi - lo) // UNROLL

    def many(i, state):
        start = lo + i * UNROLL
        for k in range(UNROLL):
            state = step(start + k, state)
        return state

    state = lax.fori_loop(0, groups, many, state)
    return lax.fori_loop(lo + groups * UNROLL, hi, step, state)


def ends_kernel(
    lens_ref, own_ref, k_ref, v_ref, rate_ref, u_ref, end_ref, span_ref, base_ref, coef_ref,
    decay_sc, state_sc, *, tok, sub, poles, count, chunk,
):
    rate = rate_ref[...]
    spread(jnp.exp(-rate), decay_sc, sub)

    def mix(i, _):
        start = pl.multiple_of(i * chunk, chunk)
        u = k_ref[pl.ds(start, chunk), :].astype(F32) * v_ref[pl.ds(start, chunk), :].astype(F32)
        spread(u, u_ref, sub, start * sub)
        return 0

    lax.fori_loop(0, tok // chunk, mix, 0)
    decay = [decay_sc[p * sub : (p + 1) * sub, :] for p in range(poles)]

    def step(t, state):
        u = u_ref[pl.ds(pl.multiple_of(t * sub, sub), sub), :]
        return tuple(d * s + u for d, s in zip(decay, state))

    base_ref[...] = jnp.zeros_like(base_ref)
    coef_ref[...] = jnp.zeros_like(coef_ref)
    span_ref[...] = jnp.zeros_like(span_ref)
    zero = tuple(jnp.zeros((sub, LANES), F32) for _ in range(poles))
    for r, (lo, hi, before, reaches, ends, steps) in enumerate(spans(lens_ref, count, tok)):

        @pl.when(hi > lo)
        def _():
            state = walk(lo, hi, step, zero)
            for p in range(poles):
                state_sc[p * sub : (p + 1) * sub, :] = state[p]

            @pl.when(hi == tok)
            def _():
                unspread(state_sc, end_ref, poles, sub)

            @pl.when(ends)
            def _():
                unspread(state_sc, base_ref.at[own_ref[r]], poles, sub)

            @pl.when(before & ends)
            def _():
                coef_ref[own_ref[r]] = jnp.exp(rate * -steps.astype(F32))

            @pl.when(before & (hi == tok))
            def _():
                span_ref[...] = jnp.exp(rate * -float(tok))


def conv_kernel(
    lens_ref, end_ref, span_ref, base_ref, coef_ref, rate_ref, res_ref, gain_ref, u_hbm, q_hbm,
    out_hbm, got_ref,
    arrived, passed, slotted, landed, decay_sc, res_sc, state_sc, gain_sc, conv_sc,
    u_ref, q_ref, out_ref, sent_sem, come_sem, give_sem, take_sem, load_sem, store_sem,
    *, hops, parts, tok, sub, poles, count, chunk, tiles,
):
    slots, _, channels = base_ref.shape
    width = channels // parts
    wide = sub * LANES
    rows_in = tok * sub
    me = lax.axis_index("ctx")
    barrier = pltpu.get_barrier_semaphore()
    peers = [lax.rem(me + j, slots) for j in range(1, slots)]
    for peer in peers:
        pl.semaphore_signal(
            barrier, inc=1, device_id={"ctx": peer}, device_id_type=pl.DeviceIdType.MESH
        )
    loads = []
    for i in range(tiles):
        flat, cols = pl.ds(i * rows_in, rows_in), pl.ds(i * wide, wide)
        loads.append(
            (
                pltpu.make_async_copy(u_hbm.at[flat, :], u_ref.at[flat, :], load_sem.at[i, 0]),
                pltpu.make_async_copy(q_hbm.at[:, cols], q_ref.at[:, cols], load_sem.at[i, 1]),
            )
        )
        loads[i][0].start()
        loads[i][1].start()
    pl.semaphore_wait(barrier, slots - 1)

    def lanes(part):
        return pl.ds(part * width, width)

    def pass_on(hop, part):
        source = end_ref if hop == 0 else passed.at[hop - 1]
        return pltpu.make_async_remote_copy(
            src_ref=source.at[:, lanes(part)],
            dst_ref=arrived.at[hop, :, lanes(part)],
            send_sem=sent_sem.at[hop, part],
            recv_sem=come_sem.at[hop, part],
            device_id={"ctx": lax.rem(me + 1, slots)},
            device_id_type=pl.DeviceIdType.MESH,
        )

    def give(j, part):
        return pltpu.make_async_remote_copy(
            src_ref=slotted.at[j - 1, :, lanes(part)],
            dst_ref=landed.at[j - 1, :, lanes(part)],
            send_sem=give_sem.at[j - 1, part],
            recv_sem=take_sem.at[j - 1, part],
            device_id={"ctx": peers[j - 1]},
            device_id_type=pl.DeviceIdType.MESH,
        )

    def arrive(hop, part):
        @pl.when(me > 0)
        def _():
            pass_on(hop, part).wait_recv()

    def hop_on(hop, part):
        if hop:
            arrive(hop - 1, part)
            at = lanes(part)
            passed[hop - 1, :, at] = span_ref[:, at] * arrived[hop - 1, :, at] + end_ref[:, at]

        @pl.when(me < slots - 1)
        def _():
            pass_on(hop, part).start()

    def finish(part):
        arrive(hops - 1, part)
        at = lanes(part)
        incoming = arrived[hops - 1, :, at]
        for j in range(1, slots):
            slotted[j - 1, :, at] = (
                base_ref[peers[j - 1], :, at] + coef_ref[peers[j - 1], :, at] * incoming
            )
            give(j, part).start()
        got_ref[0, :, at] = base_ref[me, :, at] + coef_ref[me, :, at] * incoming

    @pl.when(me == 0)
    def _():
        arrived[...] = jnp.zeros_like(arrived)

    for hop in range(hops):
        for part in range(parts):
            hop_on(hop, part)

    first = me * tok
    offset = jnp.int32(0)
    starts = []
    for r in range(count):
        starts.append(offset - first)
        offset = offset + lens_ref[r]

    def conv(i, begin, stop):
        scale = [res_sc[p] for p in range(poles)]
        gain = gain_sc[...]

        def many(n, state):
            for k in range(DEEP):
                t = n * DEEP + k
                keep = jnp.int32(1)
                for at in starts:
                    keep = keep - (t == at).astype(jnp.int32)
                pick = jnp.maximum(keep, 0) * poles
                rows = pl.ds(pl.multiple_of(t * sub, sub), sub)
                u = u_ref[pl.ds(pl.multiple_of(i * rows_in + t * sub, sub), sub), :]
                state = tuple(decay_sc[pick + p] * s + u for p, s in enumerate(state))
                terms = [gain * u] + [c * s for c, s in zip(scale, state)]
                while len(terms) > 1:
                    terms = [a + b for a, b in zip(terms[::2], terms[1::2])] + (
                        [terms[-1]] if len(terms) % 2 else []
                    )
                conv_sc[rows, :] = terms[0]
            return state

        state = tuple(state_sc[p] for p in range(poles))
        state = lax.fori_loop(begin // DEEP, stop // DEEP, many, state)
        for p in range(poles):
            state_sc[p] = state[p]

    def scatter(value, ref, base):
        for p in range(poles):
            for j in range(sub):
                ref[base + p, j : j + 1, :] = value[p : p + 1, j * LANES : (j + 1) * LANES]

    stores = []
    per_tile = parts // tiles
    for i in range(tiles):
        cols = slice(i * wide, (i + 1) * wide)
        rate = rate_ref[:, cols]
        decay_sc[0:poles] = jnp.zeros((poles, sub, LANES), F32)
        scatter(jnp.exp(-rate), decay_sc, poles)
        scatter(res_ref[:, cols] * jnp.sqrt(1.0 - jnp.exp(-2.0 * rate)), res_sc, 0)
        for j in range(sub):
            at = i * wide + j * LANES
            gain_sc[j : j + 1, :] = gain_ref[0:1, at : at + LANES]
        if i == 0:
            for part in range(per_tile):
                finish(part)
        scatter(arrived[hops - 1, :, cols], state_sc, 0)
        loads[i][0].wait()
        if i == 0 and tiles > 1:
            conv(i, 0, tok // 4)
            for part in range(per_tile, parts):
                finish(part)
            conv(i, tok // 4, tok)
        else:
            conv(i, 0, tok)
        loads[i][1].wait()

        def gate(n, _):
            start = pl.multiple_of(n * chunk, chunk)
            rows = pl.ds(start, chunk)
            for j in range(sub):
                at = slice(i * wide + j * LANES, i * wide + (j + 1) * LANES)
                value = conv_sc[pl.ds(start * sub + j, chunk, stride=sub), :]
                out_ref[rows, at] = (q_ref[rows, at].astype(F32) * value).astype(out_ref.dtype)
            return 0

        lax.fori_loop(0, tok // chunk, gate, 0)
        stores.append(
            pltpu.make_async_copy(
                out_ref.at[:, pl.ds(i * wide, wide)], out_hbm.at[:, pl.ds(i * wide, wide)],
                store_sem.at[i],
            )
        )
        stores[i].start()

    for part in range(parts):
        at = lanes(part)
        for j in range(1, slots):
            give(j, part).wait_recv()
        total = got_ref[0, :, at]
        for j in range(1, slots):
            total += landed[j - 1, :, at]
        got_ref[0, :, at] = total
    for part in range(parts):
        for j in range(1, slots):
            give(j, part).wait_send()

    @pl.when(me < slots - 1)
    def _():
        for hop in range(hops):
            for part in range(parts):
                pass_on(hop, part).wait_send()

    for copy in stores:
        copy.wait()


def shards(q_feat, k_feat, v_feat, pole_rate, residue, skip_gain, lengths, owners):
    tok, channels = q_feat.shape
    poles, count = pole_rate.shape[0], lengths.shape[0]
    slots = lax.axis_size("ctx")
    sub = min(ROWS, channels // LANES)
    width = sub * LANES
    tiles = channels // width
    sizes = dict(tok=tok, sub=sub, poles=poles, count=count, chunk=16)
    feat = pl.BlockSpec((tok, width), lambda i, *_: (0, i))
    pole = pl.BlockSpec((poles, width), lambda i, *_: (0, i))
    slot = pl.BlockSpec((slots, poles, width), lambda i, *_: (0, 0, i))
    flat = pl.BlockSpec((tok * sub, LANES), lambda i, *_: (i, 0))
    small = pltpu.VMEM((poles * sub, LANES), F32)
    elems = tok * channels
    mixed, end, span, base, coef = pl.pallas_call(
        functools.partial(ends_kernel, **sizes),
        grid_spec=pltpu.PrefetchScalarGridSpec(
            num_scalar_prefetch=2,
            grid=(tiles,),
            in_specs=[feat, feat, pole],
            out_specs=[flat, pole, pole, slot, slot],
            scratch_shapes=[small, small],
        ),
        out_shape=[
            jax.ShapeDtypeStruct((tiles * tok * sub, LANES), F32),
            jax.ShapeDtypeStruct((poles, channels), F32),
            jax.ShapeDtypeStruct((poles, channels), F32),
            jax.ShapeDtypeStruct((slots, poles, channels), F32),
            jax.ShapeDtypeStruct((slots, poles, channels), F32),
        ],
        cost_estimate=pl.CostEstimate(
            flops=2 * poles * elems, bytes_accessed=8 * elems, transcendentals=0
        ),
        name="ends",
    )(lengths, owners, k_feat, v_feat, pole_rate)

    longest = tok * slots // 2
    hops = min((longest - 2) // tok + 1, slots - 1)
    parts = max(tiles, min(4, channels // LANES))
    dma = pltpu.SemaphoreType.DMA
    vmem, hbm = pl.BlockSpec(memory_space=pltpu.VMEM), pl.BlockSpec(memory_space=pl.ANY)
    mixed_out, decode_state = pl.pallas_call(
        functools.partial(conv_kernel, hops=hops, parts=parts, tiles=tiles, **sizes),
        in_specs=[pl.BlockSpec(memory_space=pltpu.SMEM)] + [vmem] * 7 + [hbm] * 2,
        out_specs=[hbm, vmem],
        out_shape=[
            jax.ShapeDtypeStruct((tok, channels), q_feat.dtype),
            jax.ShapeDtypeStruct((1, poles, channels), F32),
        ],
        scratch_shapes=[
            pltpu.VMEM((hops, poles, channels), F32),
            pltpu.VMEM((max(hops - 1, 1), poles, channels), F32),
            pltpu.VMEM((slots - 1, poles, channels), F32),
            pltpu.VMEM((slots - 1, poles, channels), F32),
            pltpu.VMEM((2 * poles, sub, LANES), F32),
            pltpu.VMEM((poles, sub, LANES), F32),
            pltpu.VMEM((poles, sub, LANES), F32),
            pltpu.VMEM((sub, LANES), F32),
            pltpu.VMEM((tok * sub, LANES), F32),
            pltpu.VMEM((tiles * tok * sub, LANES), F32),
            pltpu.VMEM((tok, channels), q_feat.dtype),
            pltpu.VMEM((tok, channels), q_feat.dtype),
            dma((hops, parts)), dma((hops, parts)),
            dma((slots - 1, parts)), dma((slots - 1, parts)),
            dma((tiles, 2)), dma((tiles,)),
        ],
        compiler_params=pltpu.CompilerParams(collective_id=0, has_side_effects=True),
        name="conv",
    )(
        lengths, end, span, base, coef, pole_rate, residue, skip_gain[None, :], mixed, q_feat
    )
    return mixed_out, decode_state


def solution(mesh):
    tokens = P(("groups", "ctx"), "chan")
    return jax.shard_map(
        shards,
        mesh=mesh,
        in_specs=(
            tokens, tokens, tokens, P(None, "chan"), P(None, "chan"), P("chan"),
            P("groups"), P("groups"),
        ),
        out_specs=(tokens, P(("groups", "ctx"), None, "chan")),
        check_vma=False,
    )
```
